32 devices in a mesh: dp: 8 (over z, y), tensor: 4 (over x, core).
Axes of the slice: x: 2, y: 2, z: 4, core: 2. Of those that a mesh axis runs over, the one named last changes fastest.
Arguments:
- layer_in: bfloat16 [8192, 2048], P(('dp', 'tensor')), may hold values from -6 to 6
- cotangent: bfloat16 [8192, 2048], P(('dp', 'tensor')), may hold values from -6 to 6
- segments: int32 [8, 1024], P('dp'), may hold values from 0 to 3, never falling along the last dimension, each value on 1 to 800 neighbouring positions
- gain_attn: bfloat16 [2048], replicated, may hold values from 0.099609375 to 1.8984375
- w_query: bfloat16 [2048, 2048], P(None, 'tensor'), may hold values from -0.5 to 0.5
- key_weight: bfloat16 [2048, 512], P(None, 'tensor'), may hold values from -0.5 to 0.5
- value_weight: bfloat16 [2048, 512], P(None, 'tensor'), may hold values from -0.125 to 0.125
- w_out: bfloat16 [2048, 2048], P('tensor'), may hold values from -1 to 1
- gain_ffn: bfloat16 [2048], replicated, may hold values from 0.099609375 to 1.8984375
- w_gate: bfloat16 [2048, 8192], P(None, 'tensor'), may hold values from -0.125 to 0.125
- w_up: bfloat16 [2048, 8192], P(None, 'tensor'), may hold values from -0.125 to 0.125
- w_down: bfloat16 [8192, 2048], P('tensor'), may hold values from -0.25 to 0.25
Outputs:
- layer_out: bfloat16 [8192, 2048], P(('dp', 'tensor'))
- grad_in: bfloat16 [8192, 2048], P(('dp', 'tensor'))
- grad_gain_attn: float32 [2048], P('dp')
- grad_query: float32 [2048, 2048], P('dp', 'tensor')
- grad_key: float32 [2048, 512], P('dp', 'tensor')
- grad_value: float32 [2048, 512], P('dp', 'tensor')
- grad_out: float32 [2048, 2048], P('tensor', 'dp')
- grad_gain_ffn: float32 [2048], P('dp')
- grad_gate: float32 [2048, 8192], P('dp', 'tensor')
- grad_up: float32 [2048, 8192], P('dp', 'tensor')
- grad_down: float32 [8192, 2048], P('tensor', 'dp')
The draws below stay inside these ranges and needn't reach their ends.
Inputs may be any that keep to these rules, and one draw needn't show every extreme that they name: `segments`: within each sequence the numbers never fall; a document holds at most 800 tokens and some document holds exactly 800.
All inputs are finite; a program needn't handle non-finite values.
Results may differ from the reference program's by a relative error of at most 0.023.
Values may be sent and summed in bfloat16 or wider, within the bound.
A program may use at most 320 MiB of HBM per device.

```python
import math
import jax
import jax.numpy as jnp
import numpy as np
from jax import lax

MODEL_WIDTH = 2048
QUERY_HEADS = 32
KEY_VALUE_HEADS = 8
HEAD_SIZE = 64
FF = 8192
PACKED_LENGTH = 1024
DOCS = 4
DOC_MOST = 800
SEQUENCE_COUNT = 8
TOKENS = 8192


def spiked(array, own_key, source, target, parts, factor):
    owner, partner = [(jnp.arange(array.shape[axis_at]) // (array.shape[axis_at] // parts)).reshape([-1 if axis == axis_at else 1 for axis in range(array.ndim)]) for axis_at in (source, target)]
    chosen = jax.random.permutation(own_key, parts)[partner]
    strong = (owner == chosen) | (owner == (partner + parts // 2) % parts)
    return jnp.where(strong, factor * array, array)


def steps_of(key, extent, pieces, least, largest):
    def one(axis_at, blocks):
        draws = jax.random.uniform(jax.random.fold_in(jax.random.fold_in(key, 6), axis_at), (blocks,), jnp.float32, least / len(pieces), largest / len(pieces))
        return jnp.repeat(jnp.exp(draws), extent[axis_at] // blocks).reshape((-1,) + (1,) * (len(extent) - axis_at - 1))

    factor_of = one(*pieces[0])
    for cut in pieces[1:]:
        factor_of = factor_of * one(*cut)
    return factor_of


def profile(number_of, total, reach, lean):
    portions = [(1 << 20) // math.isqrt(grade ** lean) + 1 for grade in range(2, number_of + 1)]
    spare, counts = total - reach - (number_of - 1), [1] * (number_of - 1)
    while spare > 0:
        movable = [i for i in range(number_of - 1) if counts[i] < reach]
        whole, budget = sum([portions[i] for i in movable]), spare
        for i in movable:
            extra = min(reach - counts[i], max(1, budget * portions[i] // whole), spare)
            counts[i] = counts[i] + extra
            spare = spare - extra
    return np.array([reach] + counts)


def uneven_parts(stream_key, count, total, most, slope):
    if count == 2:
        one = jax.random.randint(stream_key, (), max(1, total - most), min(most, total - 1) + 1)
        return jnp.stack([one, total - one])
    tallies = jnp.asarray(profile(count, total, most, slope), jnp.int32)
    couples = (count - 1) // 2
    donor, receiver = tallies[1:1 + 2 * couples:2], tallies[2:2 + 2 * couples:2]
    room = jnp.minimum(donor - 1, most - receiver)
    shifted = jax.random.randint(jax.random.fold_in(stream_key, 1), (couples,), 0, 1 << 20) % (room + 1)
    tallies = tallies.at[1:1 + 2 * couples:2].set(donor - shifted).at[2:2 + 2 * couples:2].set(receiver + shifted)
    return tallies[jax.random.permutation(jax.random.fold_in(stream_key, 2), count)]


def scatter_about(own_key, shape, deviation, most, pieces=(), kind=jnp.bfloat16):
    entries = jax.random.normal(own_key, shape, jnp.float32) * deviation
    if len(pieces) > 0:
        entries = steps_of(own_key, shape, pieces, -0.22, 0.18) * entries
    return jnp.clip(entries, min=-most, max=most).astype(kind)


def heavy_noise(rng, extent, width, most, shards, heavy, held_as=jnp.bfloat16):
    values = width * jax.random.normal(rng, extent, jnp.float32)
    if shards:
        values = values * steps_of(rng, extent, shards, -0.22, 0.18)
    return jnp.clip(spiked(values, jax.random.fold_in(rng, 3), *heavy), -most, most).astype(held_as)


def setup_inputs(seed: int = 0) -> dict:
    keys = jax.random.split(jax.random.key(seed), 13)
    return {
        "layer_in": scatter_about(keys[0], (TOKENS, MODEL_WIDTH), 1.0, 6.0, ((0, 32),)),
        "cotangent": heavy_noise(keys[1], (TOKENS, MODEL_WIDTH), 1.0, 6.0, ((0, 32),), (0, 1, 32, 2.75)),
        "segments": jax.vmap(lambda own: jnp.searchsorted(jnp.cumsum(uneven_parts(own, DOCS, PACKED_LENGTH, DOC_MOST, 0)), jnp.arange(PACKED_LENGTH), side="right"))(jax.random.split(keys[2], SEQUENCE_COUNT)).reshape((SEQUENCE_COUNT, PACKED_LENGTH)).astype(jnp.int32),
        "gain_attn": jnp.clip(1.0 + 0.18 * jax.random.normal(keys[3], (MODEL_WIDTH,), jnp.float32), 0.099609375, 1.8984375).astype(jnp.bfloat16),
        "w_query": scatter_about(keys[4], (MODEL_WIDTH, QUERY_HEADS * HEAD_SIZE), (MODEL_WIDTH // 16) ** -0.5, 0.5, ((1, 4),)),
        "key_weight": scatter_about(keys[5], (MODEL_WIDTH, KEY_VALUE_HEADS * HEAD_SIZE), (MODEL_WIDTH // 16) ** -0.5, 0.5, ((1, 4),)),
        "value_weight": scatter_about(keys[6], (MODEL_WIDTH, KEY_VALUE_HEADS * HEAD_SIZE), MODEL_WIDTH ** -0.5, 0.125, ((1, 4),)),
        "w_out": scatter_about(keys[7], (QUERY_HEADS * HEAD_SIZE, MODEL_WIDTH), (QUERY_HEADS * HEAD_SIZE // 64) ** -0.5, 1.0, ((0, 4),)),
        "gain_ffn": jnp.clip(1.0 + 0.18 * jax.random.normal(keys[8], (MODEL_WIDTH,), jnp.float32), 0.099609375, 1.8984375).astype(jnp.bfloat16),
        "w_gate": scatter_about(keys[9], (MODEL_WIDTH, FF), MODEL_WIDTH ** -0.5, 0.125, ((1, 4),)),
        "w_up": scatter_about(keys[10], (MODEL_WIDTH, FF), MODEL_WIDTH ** -0.5, 0.125, ((1, 4),)),
        "w_down": scatter_about(keys[11], (FF, MODEL_WIDTH), (FF // 16) ** -0.5, 0.25, ((0, 4),)),
    }


@jax.custom_vjp
def reduced_cast(v):
    return lax.optimization_barrier(v.astype(jnp.bfloat16)).astype(jnp.float32)

@jax.custom_vjp
def reduced_cast_backward(v):
    return v

def low_keep(v):
    return (reduced_cast(v), None)

def low_pass(kept, grad):
    return (grad,)

def back_keep(v):
    return (v, None)

def back_low(kept, grad):
    return (reduced_cast(grad),)
reduced_cast.defvjp(low_keep, low_pass)
reduced_cast_backward.defvjp(back_keep, back_low)
EPSILON = 1e-05
MULTIPLIER = 0.015625
RESIDUAL_SCALE = 0.22
THETA_BASE = 10000.0
MASK_VALUE = -1e+30

def exact_product(left, right):
    return jnp.dot(left, right, precision=lax.Precision.HIGHEST)

def rms_norm(value_rows, gain):
    return value_rows * lax.rsqrt(lax.optimization_barrier(jnp.mean(value_rows * value_rows, axis=-1, keepdims=True)) + EPSILON) * gain

def positions_of(seg_ids):
    length = seg_ids.shape[-1]
    index = jnp.broadcast_to(jnp.arange(length, dtype=jnp.int32), seg_ids.shape)
    before = jnp.concatenate([seg_ids[:, :1] - 1, seg_ids[:, :-1]], axis=1)
    starts = jnp.where(seg_ids != before, index, jnp.zeros_like(index))
    return index - lax.cummax(starts, axis=1)

def rope_tables(positions):
    half = HEAD_SIZE // 2
    freq = THETA_BASE ** (-2.0 * jnp.arange(half, dtype=jnp.float32) / HEAD_SIZE)
    angle = positions.astype(jnp.float32)[:, None] * freq[None, :]
    return (jnp.cos(angle), jnp.sin(angle))

def apply_rotary(value_rows, cosine_table, sine_table):
    half = HEAD_SIZE // 2
    first = value_rows[..., :half]
    second = value_rows[..., half:]
    cos_b = cosine_table[:, None, :]
    sin_b = sine_table[:, None, :]
    return jnp.concatenate([first * cos_b - second * sin_b, second * cos_b + first * sin_b], axis=-1)

def attend_one(items):
    query_rows, key_rows, value_rows, seg_ids = items
    length = seg_ids.shape[0]
    raw = jnp.einsum('qhgd,khd->hgqk', query_rows, key_rows, precision=lax.Precision.HIGHEST)
    scores = reduced_cast_backward(MULTIPLIER * raw)
    index = jnp.arange(length, dtype=jnp.int32)
    allowed = (seg_ids[:, None] == seg_ids[None, :]) & (index[None, :] <= index[:, None])
    scores = jnp.where(allowed, scores, MASK_VALUE)
    top = lax.optimization_barrier(jnp.max(scores, axis=-1, keepdims=True))
    lse = top + jnp.log(lax.optimization_barrier(jnp.sum(jnp.exp(scores - top), axis=-1, keepdims=True)))
    probs = reduced_cast(jnp.exp(scores - lse))
    return jnp.einsum('hgqk,khd->qhgd', probs, value_rows, precision=lax.Precision.HIGHEST)

def forward(layer_in, gain_attn, w_query, key_weight, value_weight, w_out, gain_ffn, w_gate, w_up, w_down, cosine_table, sine_table, segments):
    token_rows = layer_in.shape[0]
    query_group = QUERY_HEADS // KEY_VALUE_HEADS
    normalized_input = reduced_cast(rms_norm(layer_in, gain_attn))
    query_rows = reduced_cast_backward(exact_product(normalized_input, w_query)).reshape(token_rows, QUERY_HEADS, HEAD_SIZE)
    key_rows = reduced_cast_backward(exact_product(normalized_input, key_weight)).reshape(token_rows, KEY_VALUE_HEADS, HEAD_SIZE)
    value_rows = reduced_cast(reduced_cast_backward(exact_product(normalized_input, value_weight))).reshape(SEQUENCE_COUNT, PACKED_LENGTH, KEY_VALUE_HEADS, HEAD_SIZE)
    rotated_query = reduced_cast(apply_rotary(query_rows, cosine_table, sine_table)).reshape(SEQUENCE_COUNT, PACKED_LENGTH, KEY_VALUE_HEADS, query_group, HEAD_SIZE)
    rotated_keys = reduced_cast(apply_rotary(key_rows, cosine_table, sine_table)).reshape(SEQUENCE_COUNT, PACKED_LENGTH, KEY_VALUE_HEADS, HEAD_SIZE)
    attended = lax.map(jax.checkpoint(attend_one), (rotated_query, rotated_keys, value_rows, segments))
    attn_low = reduced_cast(reduced_cast_backward(attended.reshape(token_rows, QUERY_HEADS * HEAD_SIZE)))
    branch = reduced_cast_backward(exact_product(attn_low, w_out))
    hidden = layer_in + RESIDUAL_SCALE * branch
    normed_two = reduced_cast(rms_norm(hidden, gain_ffn))
    gate = reduced_cast_backward(exact_product(normed_two, w_gate))
    upper = reduced_cast_backward(exact_product(normed_two, w_up))
    mixed = reduced_cast(jax.nn.silu(gate) * upper)
    ffn_out = reduced_cast_backward(exact_product(mixed, w_down))
    return hidden + RESIDUAL_SCALE * ffn_out

def reference(layer_in, cotangent, segments, gain_attn, w_query, key_weight, value_weight, w_out, gain_ffn, w_gate, w_up, w_down):
    positions = positions_of(segments).reshape(-1)
    cosine_table, sine_table = rope_tables(positions)

    def closed(*params):
        return forward(*params, cosine_table, sine_table, segments)
    params = [p.astype(jnp.float32) for p in (layer_in, gain_attn, w_query, key_weight, value_weight, w_out, gain_ffn, w_gate, w_up, w_down)]
    result, pullback = jax.vjp(closed, *params)
    grads = pullback(cotangent.astype(jnp.float32))
    return (result.astype(jnp.bfloat16), grads[0].astype(jnp.bfloat16), grads[1], grads[2], grads[3], grads[4], grads[5], grads[6], grads[7], grads[8], grads[9])
```

```python
import functools

import jax
import jax.numpy as jnp
from jax import lax
from jax.experimental import pallas as pl
from jax.experimental.pallas import tpu as pltpu
from jax.sharding import PartitionSpec as P

HEAD_SIZE = 64


EPSILON = 1e-05
MULTIPLIER = 0.015625
RESIDUAL_SCALE = 0.22
THETA_BASE = 10000.0
MASK_VALUE = -1e30
LOW = jnp.bfloat16
WIDE = jnp.float32
LANES = 128
TILE = 256
NN = (((1,), (0,)), ((), ()))
NT = (((1,), (1,)), ((), ()))
TN = (((0,), (0,)), ((), ()))


def dot(a, b, dims=NN):
    return lax.dot_general(a, b, dims, preferred_element_type=WIDE)


def after(value, *others):
    return lax.optimization_barrier((value, *others))[0]


def positions_of(seg_ids):
    length = seg_ids.shape[-1]
    index = jnp.broadcast_to(jnp.arange(length, dtype=jnp.int32), seg_ids.shape)
    before = jnp.concatenate([seg_ids[:, :1] - 1, seg_ids[:, :-1]], axis=1)
    starts = jnp.where(seg_ids != before, index, jnp.zeros_like(index))
    return index - lax.cummax(starts, axis=1)


def rope_tables(positions):
    half = HEAD_SIZE // 2
    freq = THETA_BASE ** (-2.0 * jnp.arange(half, dtype=jnp.float32) / HEAD_SIZE)
    angle = positions.astype(jnp.float32)[:, None] * freq[None, :]
    cosine, sine = jnp.cos(angle), jnp.sin(angle)
    repeats = LANES // HEAD_SIZE
    return (
        jnp.concatenate([cosine, cosine] * repeats, axis=1),
        jnp.concatenate([-sine, sine] * repeats, axis=1),
    )


def lane_index(shape):
    return lax.broadcasted_iota(jnp.int32, shape, len(shape) - 1)


def turn(u, cosine, sine):
    quarter = HEAD_SIZE // 2
    first = lane_index(u.shape) % HEAD_SIZE < quarter
    other = jnp.where(
        first, pltpu.roll(u, u.shape[1] - quarter, 1), pltpu.roll(u, quarter, 1)
    )
    return u * cosine + other * sine


def project_kernel(turned, n_ref, w_ref, cos_ref, sin_ref, out_ref):
    cosine, sine = cos_ref[...], sin_ref[...]
    out = dot(n_ref[...], w_ref[...])
    for j in range(out.shape[1] // LANES):
        part = out[:, j * LANES : (j + 1) * LANES]
        if j * LANES < turned:
            part = turn(part, cosine, sine)
        out_ref[:, j * LANES : (j + 1) * LANES] = part.astype(LOW)


def project(n, weight, cosine, sine, turned):
    rows, width = n.shape
    columns = weight.shape[1]
    moving = lambda i: (i, 0)
    return pl.pallas_call(
        functools.partial(project_kernel, turned),
        grid=(rows // TILE,),
        in_specs=[
            pl.BlockSpec((TILE, width), moving),
            pl.BlockSpec((width, columns), lambda i: (0, 0)),
            pl.BlockSpec((TILE, LANES), moving),
            pl.BlockSpec((TILE, LANES), moving),
        ],
        out_specs=pl.BlockSpec((TILE, columns), moving),
        out_shape=jax.ShapeDtypeStruct((rows, columns), LOW),
        cost_estimate=pl.CostEstimate(
            flops=2 * rows * width * columns,
            bytes_accessed=2 * (rows * width + width * columns + rows * columns),
            transcendentals=0,
        ),
        name="project",
    )(n, weight, cosine, sine)


def doubled(pair, half):
    swapped = pltpu.roll(pair.astype(WIDE), HEAD_SIZE, 1).astype(pair.dtype)
    low = lane_index(pair.shape) < HEAD_SIZE
    return jnp.where(low == (half == 0), pair, swapped)


def attend_kernel(per_kv, q_ref, k_ref, v_ref, segq_ref, segk_ref, o_ref, lse_ref):
    half = (pl.program_id(1) // per_kv) % 2
    length = k_ref.shape[0]
    k, v = doubled(k_ref[...], half), doubled(v_ref[...], half)
    low = lane_index((TILE, LANES)) < HEAD_SIZE
    q_at = lax.broadcasted_iota(jnp.int32, (TILE, TILE), 0)
    k_at = lax.broadcasted_iota(jnp.int32, (TILE, TILE), 1)
    for i in range(length // TILE):
        rows = slice(i * TILE, (i + 1) * TILE)
        reach = (i + 1) * TILE
        q = q_ref[rows, :]
        same = segq_ref[rows, :] == segk_ref[:, :reach]
        last = same[:, i * TILE :] & (k_at <= q_at)
        allowed = jnp.concatenate([same[:, : i * TILE], last], axis=1) if i else last
        outs = []
        for head in range(2):
            mine = jnp.where(low == (head == 0), q, jnp.zeros_like(q))
            raw = dot(mine, k[:reach], NT)
            scores = jnp.where(allowed, MULTIPLIER * raw, MASK_VALUE)
            top = jnp.max(scores, axis=1, keepdims=True)
            e = jnp.exp(scores - top)
            total = jnp.sum(e, axis=1, keepdims=True)
            p = (e * (1.0 / total)).astype(LOW)
            outs.append(dot(p, v[:reach]))
            lse = top + jnp.log(total)
            lse_ref[0, head : head + 1, rows] = jnp.transpose(
                jnp.broadcast_to(lse, (TILE, LANES))
            )[:1]
        o_ref[rows, :] = jnp.where(low, outs[0], outs[1]).astype(LOW)


def attend(qkv, q_width, kv_width, seg_col, seg_row, seqs):
    rows = qkv.shape[0]
    length = rows // seqs
    pairs, kv_pairs = q_width // LANES, kv_width // LANES
    per_kv = pairs // kv_pairs // 2
    return pl.pallas_call(
        functools.partial(attend_kernel, per_kv),
        grid=(seqs, pairs),
        in_specs=[
            pl.BlockSpec((length, LANES), lambda s, h: (s, h)),
            pl.BlockSpec((length, LANES), lambda s, h: (s, pairs + h // (2 * per_kv))),
            pl.BlockSpec((length, LANES), lambda s, h: (s, pairs + kv_pairs + h // (2 * per_kv))),
            pl.BlockSpec((length, 1), lambda s, h: (s, 0)),
            pl.BlockSpec((None, 1, length), lambda s, h: (s, 0, 0)),
        ],
        out_specs=[
            pl.BlockSpec((length, LANES), lambda s, h: (s, h)),
            pl.BlockSpec((1, 2, length), lambda s, h: (h, 0, s)),
        ],
        out_shape=[
            jax.ShapeDtypeStruct((rows, q_width), LOW),
            jax.ShapeDtypeStruct((pairs, 2, rows), WIDE),
        ],
        cost_estimate=pl.CostEstimate(
            flops=4 * rows * length * q_width,
            bytes_accessed=6 * rows * q_width,
            transcendentals=rows * length * pairs * 2,
        ),
        name="attend",
    )(qkv, qkv, qkv, seg_col, seg_row)


def attend_back_kernel(
    per_kv,
    q_ref,
    k_ref,
    v_ref,
    g_ref,
    lse_ref,
    segc_ref,
    segr_ref,
    cos_ref,
    sin_ref,
    dq_ref,
    dk_ref,
    dv_ref,
    dk_acc,
    dv_acc,
    p_buf,
    dp_buf,
):
    pair = pl.program_id(1)
    slot = (pair // per_kv) % 2
    length = k_ref.shape[0]
    k, v = doubled(k_ref[...], slot), doubled(v_ref[...], slot)
    low = lane_index((TILE, LANES)) < HEAD_SIZE
    k_at = lax.broadcasted_iota(jnp.int32, (TILE, TILE), 0)
    q_at = lax.broadcasted_iota(jnp.int32, (TILE, TILE), 1)

    @pl.when(pair % per_kv == 0)
    def _():
        dk_acc[slot] = jnp.zeros_like(dk_acc[slot])
        dv_acc[slot] = jnp.zeros_like(dv_acc[slot])

    for i in range(length // TILE):
        rows = slice(i * TILE, (i + 1) * TILE)
        q, g = q_ref[rows, :], g_ref[rows, :]
        dq = []
        for head in range(2):
            chosen = low == (head == 0)
            qh = jnp.where(chosen, q, jnp.zeros_like(q))
            gh = jnp.where(chosen, g, jnp.zeros_like(g))
            lse = lse_ref[0, head : head + 1, rows]
            inner = jnp.zeros((1, TILE), WIDE)
            for j in range(i + 1):
                keys = slice(j * TILE, (j + 1) * TILE)
                allowed = segc_ref[keys, :] == segr_ref[:, rows]
                if i == j:
                    allowed = allowed & (k_at <= q_at)
                raw = dot(k[keys], qh, NT)
                p = jnp.exp(jnp.where(allowed, MULTIPLIER * raw, MASK_VALUE) - lse)
                dp = dot(v[keys], gh, NT)
                inner = inner + jnp.sum(p * dp, axis=0, keepdims=True)
                p_buf[keys, :] = p
                dp_buf[keys, :] = dp
            total = jnp.zeros((TILE, LANES), WIDE)
            for j in range(i + 1):
                keys = slice(j * TILE, (j + 1) * TILE)
                p = p_buf[keys, :]
                ds = (p * (dp_buf[keys, :] - inner)).astype(LOW)
                dv_acc[slot, keys, :] += dot(p.astype(LOW), gh)
                dk_acc[slot, keys, :] += dot(ds, qh)
                total = total + dot(ds, k[keys], TN)
            dq.append(total)
        dq_ref[rows, :] = turn(
            MULTIPLIER * jnp.where(low, dq[0], dq[1]), cos_ref[rows, :], -sin_ref[rows, :]
        ).astype(LOW)

    @pl.when(pair % (2 * per_kv) == 2 * per_kv - 1)
    def _():
        low_all = lane_index((length, LANES)) < HEAD_SIZE

        def folded(acc):
            a, b = acc[0], acc[1]
            a = a + pltpu.roll(a, HEAD_SIZE, 1)
            b = b + pltpu.roll(b, HEAD_SIZE, 1)
            return jnp.where(low_all, a, b)

        dk_ref[...] = turn(MULTIPLIER * folded(dk_acc), cos_ref[...], -sin_ref[...]).astype(LOW)
        dv_ref[...] = folded(dv_acc).astype(LOW)


def attend_back(qkv, q_width, kv_width, g, lse, seg_col, seg_row, cosine, sine, seqs):
    rows = qkv.shape[0]
    length = rows // seqs
    pairs, kv_pairs = q_width // LANES, kv_width // LANES
    per_kv = pairs // kv_pairs // 2
    by_pair = lambda s, h: (s, h)
    by_kv = lambda s, h: (s, h // (2 * per_kv))
    by_seq = lambda s, h: (s, 0)
    return pl.pallas_call(
        functools.partial(attend_back_kernel, per_kv),
        grid=(seqs, pairs),
        in_specs=[
            pl.BlockSpec((length, LANES), by_pair),
            pl.BlockSpec((length, LANES), lambda s, h: (s, pairs + h // (2 * per_kv))),
            pl.BlockSpec((length, LANES), lambda s, h: (s, pairs + kv_pairs + h // (2 * per_kv))),
            pl.BlockSpec((length, LANES), by_pair),
            pl.BlockSpec((1, 2, length), lambda s, h: (h, 0, s)),
            pl.BlockSpec((length, 1), by_seq),
            pl.BlockSpec((None, 1, length), lambda s, h: (s, 0, 0)),
            pl.BlockSpec((length, LANES), by_seq),
            pl.BlockSpec((length, LANES), by_seq),
        ],
        out_specs=[
            pl.BlockSpec((length, LANES), by_pair),
            pl.BlockSpec((length, LANES), by_kv),
            pl.BlockSpec((length, LANES), by_kv),
        ],
        out_shape=[
            jax.ShapeDtypeStruct((rows, q_width), LOW),
            jax.ShapeDtypeStruct((rows, kv_width), LOW),
            jax.ShapeDtypeStruct((rows, kv_width), LOW),
        ],
        scratch_shapes=[
            pltpu.VMEM((2, length, LANES), WIDE),
            pltpu.VMEM((2, length, LANES), WIDE),
            pltpu.VMEM((length, TILE), WIDE),
            pltpu.VMEM((length, TILE), WIDE),
        ],
        cost_estimate=pl.CostEstimate(
            flops=10 * rows * length * q_width,
            bytes_accessed=10 * rows * q_width,
            transcendentals=rows * length * pairs * 2,
        ),
        name="attend_back",
    )(qkv, qkv, qkv, g, lse, seg_col, seg_row, cosine, sine)


def mix_kernel(n_ref, wg_ref, wu_ref, dm_ref, *refs):
    m_ref, dg_ref, du_ref = refs[-3:]
    n = n_ref[...]
    g = dot(n, wg_ref[...])
    u = dot(n, wu_ref[...])
    dm = dm_ref[...]
    s = jax.nn.sigmoid(g)
    active = g * s
    m_ref[...] = (active * u).astype(LOW)
    dg_ref[...] = (dm * u * s * (1.0 + g * (1.0 - s))).astype(LOW)
    du_ref[...] = (dm * active).astype(LOW)


def mix(n, wg, wu, dm, at, held=()):
    rows, width = n.shape
    units = wg.shape[1]
    moving = lambda i: (0, i)
    spec = pl.BlockSpec((rows, TILE), lambda i: (at, i))
    return pl.pallas_call(
        mix_kernel,
        grid=(units // TILE,),
        in_specs=[
            pl.BlockSpec((rows, width), lambda i: (0, 0)),
            pl.BlockSpec((width, TILE), moving),
            pl.BlockSpec((width, TILE), moving),
            spec,
        ]
        + [pl.BlockSpec(memory_space=pl.ANY)] * len(held),
        out_specs=[spec] * 3,
        out_shape=[jax.ShapeDtypeStruct(dm.shape, LOW)] * 3,
        input_output_aliases={4 + i: i for i in range(len(held))},
        cost_estimate=pl.CostEstimate(
            flops=4 * rows * width * units,
            bytes_accessed=4 * width * units + 2 * rows * width + 10 * rows * units,
            transcendentals=rows * units,
        ),
        name="mix",
    )(n, wg, wu, dm, *held)


def unmix_kernel(dg_ref, du_ref, wg_ref, wu_ref, *out_refs):
    total = dot(dg_ref[...], wg_ref[...], NT) + dot(du_ref[...], wu_ref[...], NT)
    share = out_refs[0].shape[0]
    for i, ref in enumerate(out_refs):
        ref[...] = total[i * share : (i + 1) * share].astype(LOW)


def unmix(dg, du, wg, wu, at, share, pieces):
    units, width = dg.shape[1], wg.shape[0]
    rows = share * pieces
    held = pl.BlockSpec((rows, units), lambda i: (at, 0))
    moving = pl.BlockSpec((TILE, units), lambda i: (i, 0))
    return pl.pallas_call(
        unmix_kernel,
        grid=(width // TILE,),
        in_specs=[held, held, moving, moving],
        out_specs=[pl.BlockSpec((share, TILE), lambda i: (0, i))] * pieces,
        out_shape=[jax.ShapeDtypeStruct((share, width), LOW)] * pieces,
        cost_estimate=pl.CostEstimate(
            flops=4 * rows * width * units,
            bytes_accessed=4 * width * units + 4 * rows * units + 2 * rows * width,
            transcendentals=0,
        ),
        name="unmix",
    )(dg, du, wg, wu)


def swap(array, axis, mask):
    size = lax.axis_size(axis)
    return lax.ppermute(array, axis, [(i, i ^ mask) for i in range(size)])


def powers(size):
    return [1 << i for i in range(size.bit_length() - 1)]


def spread_masks(size):
    masks, bit = [1], 2
    while bit < size:
        masks.append(bit)
        if 2 * bit < size:
            masks.append(3 * bit)
        bit *= 4
    return masks


def gather_shares(own):
    shares = {0: own}
    for mask in reversed(powers(lax.axis_size("tensor"))):
        shares.update({r ^ mask: swap(a, "tensor", mask) for r, a in shares.items()})
    return [shares[r] for r in range(len(shares))]


def sum_shares(parts):
    parts = dict(enumerate(parts))
    for mask in powers(lax.axis_size("tensor")):
        sent = {r: a for r, a in parts.items() if r & mask}
        parts = {r: a for r, a in parts.items() if not r & mask}
        for r, a in reversed(sent.items()):
            got = swap(a.astype(LOW), "tensor", mask).astype(WIDE)
            parts[r ^ mask] = parts[r ^ mask].astype(WIDE) + got
    return parts[0]


def in_order(shares, rank):
    share = shares[0].shape[0]
    whole = jnp.zeros((share * len(shares),) + shares[0].shape[1:], shares[0].dtype)
    for r, a in enumerate(shares):
        whole = lax.dynamic_update_slice_in_dim(whole, a, (rank ^ r) * share, 0)
    return whole


def out_of_order(whole, rank):
    count = lax.axis_size("tensor")
    share = whole.shape[0] // count
    return [lax.dynamic_slice_in_dim(whole, (rank ^ r) * share, share, 0) for r in range(count)]


def block_order(masks):
    order = [0]
    for mask in reversed(masks):
        order = [mask ^ b for b in order] + order
    return order


def permute_columns(array, masks, place):
    count = 1 << len(masks)
    width = array.shape[1] // count
    return jnp.concatenate(
        [
            lax.dynamic_slice_in_dim(array, (place ^ b) * width, width, 1)
            for b in block_order(masks)
        ],
        axis=1,
    )


class Reduction:
    def __init__(self, term, masks, width, axis):
        self.term, self.masks, self.width, self.axis = term, list(masks), width, axis
        self.count = 1 << len(masks)
        self.low, self.size, self.got = 0, self.count // 2, []
        self.sent = None

    def total(self, low, high):
        value = self.term(low, high)
        for first, array in self.got:
            piece = lax.slice_in_dim(
                array, (low - first) * self.width, (high - first) * self.width, axis=self.axis
            )
            value = value + piece.astype(WIDE)
        return value

    def step(self):
        self.sent = self.total(self.low, self.low + self.size).astype(LOW)
        self.low += self.size
        self.size //= 2
        self.got.append((self.low, swap(self.sent, "dp", self.masks.pop(0))))
        return self

    def finish(self):
        while self.masks:
            self.step()
        return self.total(self.low, self.count)


def reduce_rows(left, right, masks):
    width = left.shape[1] // (1 << len(masks))
    term = lambda low, high: dot(left[:, low * width : high * width], right, TN)
    return Reduction(term, masks, width, 0)


def reduce_cols(left, right, masks):
    width = right.shape[1] // (1 << len(masks))
    term = lambda low, high: dot(left, right[:, low * width : high * width], TN)
    return Reduction(term, masks, width, 1)


def rotate(masks, by):
    by %= len(masks)
    return masks[by:] + masks[:by]


def rows_of(shares):
    return jnp.concatenate(shares, axis=0)


def inverse_rms(value_rows):
    return lax.rsqrt(jnp.mean(value_rows * value_rows, axis=-1, keepdims=True) + EPSILON)


def norm_back(d_normed, value_rows, inverse, gain):
    scaled = d_normed * gain
    return inverse * scaled - value_rows * inverse**3 * jnp.mean(
        scaled * value_rows, axis=-1, keepdims=True
    )


def body(
    layer_in,
    cotangent,
    segments,
    gain_attn,
    w_query,
    key_weight,
    value_weight,
    w_out,
    gain_ffn,
    w_gate,
    w_up,
    w_down,
):
    share, width = layer_in.shape
    count = lax.axis_size("tensor")
    half = count // 2
    rank = lax.axis_index("tensor")
    place = lax.axis_index("dp")
    masks = spread_masks(lax.axis_size("dp"))
    order_a = order_b = masks
    order_c = masks[1:2] + masks[:1] + masks[2:]
    seqs = segments.shape[0]
    q_width, kv_width = w_query.shape[1], key_weight.shape[1]

    gain_one = gain_attn.astype(WIDE)
    gain_two = gain_ffn.astype(WIDE)
    x = layer_in.astype(WIDE)
    inverse_one = inverse_rms(x)
    n1_shares = gather_shares((x * inverse_one * gain_one).astype(LOW))
    d_out = cotangent.astype(WIDE)
    branch_own = after((RESIDUAL_SCALE * d_out).astype(LOW), n1_shares[half])
    branch_shares = gather_shares(branch_own)

    w_qkv = jnp.concatenate([w_query, key_weight, value_weight], axis=1)
    cosine, sine = rope_tables(positions_of(segments).reshape(-1))
    seg_col, seg_row = segments.reshape(-1, 1), segments[:, None, :]
    cos_parts, sin_parts = out_of_order(cosine, rank), out_of_order(sine, rank)
    turned = q_width + kv_width
    qkv_shares = []
    for low in (0, half):
        part = slice(low, low + half)
        out = project(
            rows_of(n1_shares[part]), w_qkv, rows_of(cos_parts[part]), rows_of(sin_parts[part]), turned
        )
        qkv_shares += [out[i * share : (i + 1) * share] for i in range(half)]
    qkv = in_order(qkv_shares, rank)
    attended, lse = attend(qkv, q_width, kv_width, seg_col, seg_row, seqs)
    attn_shares = out_of_order(attended, rank)
    attn_parts = [dot(a, w_out).astype(LOW) for a in attn_shares]
    attn_total = sum_shares(attn_parts)

    d_branch = after(rows_of(branch_shares), *attn_parts)
    d_mixed = dot(d_branch, w_down, NT)
    hidden = x + RESIDUAL_SCALE * attn_total
    inverse_two = inverse_rms(hidden)
    n2_shares = gather_shares((hidden * inverse_two * gain_two).astype(LOW))
    held = mix(rows_of(n2_shares[:half]), w_gate, w_up, d_mixed, 0)
    mixed, d_gate, d_upper = mix(rows_of(n2_shares[half:]), w_gate, w_up, d_mixed, 1, held)

    n2 = rows_of(n2_shares)
    grad_down = reduce_cols(mixed, permute_columns(d_branch, order_a, place), order_a).step()
    grad_gate = reduce_rows(permute_columns(n2, order_b, place), d_gate, order_b).step()
    grad_up = reduce_rows(permute_columns(n2, order_c, place), d_upper, order_c).step()
    d_gate_late = after(d_gate, grad_down.sent, grad_gate.sent, grad_up.sent)
    far = unmix(d_gate_late, d_upper, w_gate, w_up, 1, share, half)
    near = unmix(after(d_gate_late, *far), d_upper, w_gate, w_up, 0, share, half)
    d_normed = sum_shares(list(near) + list(far))
    gain_two_part = jnp.sum(d_normed * hidden * inverse_two, axis=0)
    d_hidden = d_out + norm_back(d_normed, hidden, inverse_two, gain_two)
    da_shares = gather_shares((RESIDUAL_SCALE * d_hidden).astype(LOW))

    ffn_part = dot(after(mixed, *near), w_down).astype(LOW)
    ffn_part = after(ffn_part, da_shares[half])
    ffn_total = sum_shares([ffn_part[r * share : (r + 1) * share] for r in range(count)])
    out_rows = (hidden + RESIDUAL_SCALE * ffn_total).astype(LOW)

    d_attn = in_order([dot(a, w_out, NT).astype(LOW) for a in da_shares], rank)
    d_query, d_keys, d_values = attend_back(
        qkv, q_width, kv_width, d_attn, lse, seg_col, seg_row, cosine, sine, seqs
    )
    grad_wout = reduce_cols(
        rows_of(attn_shares), permute_columns(rows_of(da_shares), order_a, place), order_a
    ).step()
    n1 = rows_of(n1_shares)
    d_qkv_shares = [
        jnp.concatenate(parts, axis=1)
        for parts in zip(*(out_of_order(a, rank) for a in (d_query, d_keys, d_values)))
    ]
    d_qkv = rows_of(d_qkv_shares)
    grad_q = reduce_rows(permute_columns(n1, order_b, place), d_qkv[:, :q_width], order_b).step()
    grad_kv = reduce_rows(permute_columns(n1, order_c, place), d_qkv[:, q_width:], order_c).step()
    d_qkv_late = [after(a, grad_q.sent, grad_kv.sent) for a in d_qkv_shares]
    d_norm_parts = [dot(a, w_qkv, NT).astype(LOW) for a in d_qkv_late]
    d_normed_one = sum_shares(d_norm_parts)
    grad_rows = (d_hidden + norm_back(d_normed_one, x, inverse_one, gain_one)).astype(LOW)

    gain_one_part = sum(
        jnp.sum(d.astype(WIDE) * n.astype(WIDE), axis=0)
        for d, n in zip(d_norm_parts, [after(n, *d_norm_parts) for n in n1_shares])
    )
    gains = jnp.stack([gain_one_part / gain_one, gain_two_part])
    block = width // lax.axis_size("dp")
    gains = permute_columns(gains, masks, place)
    for mask in powers(count):
        gains = gains + swap(gains, "tensor", mask)
    gains = Reduction(
        lambda low, high: gains[:, low * block : high * block], masks, block, 1
    ).finish()
    grad_kv = grad_kv.finish()
    return (
        out_rows,
        grad_rows,
        gains[0],
        grad_q.finish(),
        grad_kv[:, :kv_width],
        grad_kv[:, kv_width:],
        grad_wout.finish(),
        gains[1],
        grad_gate.finish(),
        grad_up.finish(),
        grad_down.finish(),
    )


def solution(mesh):
    return jax.shard_map(
        body,
        mesh=mesh,
        in_specs=(
            P(("dp", "tensor"), None),
            P(("dp", "tensor"), None),
            P("dp", None),
            P(),
            P(None, "tensor"),
            P(None, "tensor"),
            P(None, "tensor"),
            P("tensor", None),
            P(),
            P(None, "tensor"),
            P(None, "tensor"),
            P("tensor", None),
        ),
        out_specs=(
            P(("dp", "tensor"), None),
            P(("dp", "tensor"), None),
            P("dp"),
            P("dp", "tensor"),
            P("dp", "tensor"),
            P("dp", "tensor"),
            P("tensor", "dp"),
            P("dp"),
            P("dp", "tensor"),
            P("dp", "tensor"),
            P("tensor", "dp"),
        ),
        check_vma=False,
    )
```

```python
import functools

import jax
import jax.numpy as jnp
from jax import lax
from jax.experimental import pallas as pl
from jax.experimental.pallas import tpu as pltpu
from jax.sharding import PartitionSpec as P

HEAD_SIZE = 64


EPSILON = 1e-05
MULTIPLIER = 0.015625
RESIDUAL_SCALE = 0.22
THETA_BASE = 10000.0
MASK_VALUE = -1e30
LOW = jnp.bfloat16
WIDE = jnp.float32
LANES = 128
TILE = 256
NN = (((1,), (0,)), ((), ()))
NT = (((1,), (1,)), ((), ()))
TN = (((0,), (0,)), ((), ()))
COST = pl.CostEstimate(flops=1, bytes_accessed=1, transcendentals=0)


def dot(a, b, dims=NN):
    return lax.dot_general(a, b, dims, preferred_element_type=WIDE)


def after(value, *others):
    return lax.optimization_barrier((value, *others))[0]


class Lane:
    def __init__(self):
        self.last = ()

    def __call__(self, function, *operands):
        if self.last:
            operands = after(operands, *self.last)
        result = function(*operands)
        self.last = tuple(jax.tree.leaves(result))
        return result


def positions_of(seg_ids):
    length = seg_ids.shape[-1]
    index = jnp.broadcast_to(jnp.arange(length, dtype=jnp.int32), seg_ids.shape)
    before = jnp.concatenate([seg_ids[:, :1] - 1, seg_ids[:, :-1]], axis=1)
    starts = jnp.where(seg_ids != before, index, jnp.zeros_like(index))
    return index - lax.cummax(starts, axis=1)


def rope_tables(positions):
    half = HEAD_SIZE // 2
    freq = THETA_BASE ** (-2.0 * jnp.arange(half, dtype=jnp.float32) / HEAD_SIZE)
    angle = positions.astype(jnp.float32)[:, None] * freq[None, :]
    cosine, sine = jnp.cos(angle), jnp.sin(angle)
    repeats = LANES // HEAD_SIZE
    return (
        jnp.concatenate([cosine, cosine] * repeats, axis=1),
        jnp.concatenate([-sine, sine] * repeats, axis=1),
    )


def lane_index(shape):
    return lax.broadcasted_iota(jnp.int32, shape, len(shape) - 1)


def turn(u, cosine, sine):
    quarter = HEAD_SIZE // 2
    first = lane_index(u.shape) % HEAD_SIZE < quarter
    other = jnp.where(
        first, pltpu.roll(u, u.shape[1] - quarter, 1), pltpu.roll(u, quarter, 1)
    )
    return u * cosine + other * sine


def load_shares(share_refs, held, sems):
    copies, first = [], 0
    for i, ref in enumerate(share_refs):
        copies.append(pltpu.make_async_copy(ref, held.at[pl.ds(first, ref.shape[0])], sems.at[i]))
        first += ref.shape[0]
    for copy in copies:
        copy.start()
    for copy in copies:
        copy.wait()


def rows_in(shares):
    return sum(a.shape[0] for a in shares)


def project_kernel(count, turned, dims, order_ref, *refs):
    share_refs, w_ref, tables = refs[:count], refs[count], refs[count + 1 : count + 3]
    out_ref, held, sems = refs[-3:]
    share = out_ref.shape[0]

    @pl.when(pl.program_id(0) == 0)
    def _():
        load_shares(share_refs, held, sems)

    mine = held[pl.ds(pl.multiple_of(pl.program_id(0) * share, share), share), :]
    out = dot(mine, w_ref[...], dims)
    for j in range(out.shape[1] // LANES):
        part = out[:, j * LANES : (j + 1) * LANES]
        if j * LANES < turned:
            part = turn(part, tables[0][...], tables[1][...])
        out_ref[:, j * LANES : (j + 1) * LANES] = part.astype(LOW)


def project(shares, order, weight, rows, dims, turned=0, tables=(), given=()):
    count, (share, width) = len(shares), shares[0].shape
    columns = weight.shape[1] if dims is NN else weight.shape[0]
    moving = lambda i, order: (order[i], 0)
    return pl.pallas_call(
        functools.partial(project_kernel, count, turned, dims),
        grid_spec=pltpu.PrefetchScalarGridSpec(
            num_scalar_prefetch=1,
            grid=(count,),
            in_specs=[pl.BlockSpec(memory_space=pl.ANY)] * count
            + [pl.BlockSpec(weight.shape, lambda i, order: (0, 0))]
            + [pl.BlockSpec((share, LANES), moving)] * len(tables)
            + [pl.BlockSpec(memory_space=pl.ANY)] * len(given),
            out_specs=pl.BlockSpec((share, columns), moving),
            scratch_shapes=[
                pltpu.VMEM((count * share, width), LOW),
                pltpu.SemaphoreType.DMA((count,)),
            ],
        ),
        out_shape=jax.ShapeDtypeStruct((rows, columns), LOW),
        input_output_aliases={count + 2 + len(tables): 0} if given else {},
        cost_estimate=COST,
        name="project",
    )(order, *shares, weight, *tables, *given)


def pieces_kernel(dims, order_ref, a_ref, w_ref, *out_refs):
    w = w_ref[...]
    for i, ref in enumerate(out_refs):
        share = ref.shape[0]
        mine = a_ref[pl.ds(pl.multiple_of(order_ref[i] * share, share), share), :]
        ref[...] = dot(mine, w, dims).astype(LOW)


def pieces(a, weight, order, count, transposed):
    rows, depth = a.shape
    share = rows // count
    width = weight.shape[0] if transposed else weight.shape[1]
    moving = (
        pl.BlockSpec((TILE, depth), lambda i, order: (i, 0))
        if transposed
        else pl.BlockSpec((depth, TILE), lambda i, order: (0, i))
    )
    return pl.pallas_call(
        functools.partial(pieces_kernel, NT if transposed else NN),
        grid_spec=pltpu.PrefetchScalarGridSpec(
            num_scalar_prefetch=1,
            grid=(width // TILE,),
            in_specs=[pl.BlockSpec((rows, depth), lambda i, order: (0, 0)), moving],
            out_specs=[pl.BlockSpec((share, TILE), lambda i, order: (0, i))] * count,
        ),
        out_shape=[jax.ShapeDtypeStruct((share, width), LOW)] * count,
        cost_estimate=COST,
        name="pieces",
    )(order, a, weight)


def doubled(pair, half):
    swapped = pltpu.roll(pair.astype(WIDE), HEAD_SIZE, 1).astype(pair.dtype)
    low = lane_index(pair.shape) < HEAD_SIZE
    return jnp.where(low == (half == 0), pair, swapped)


def attend_kernel(per_kv, q_ref, k_ref, v_ref, segq_ref, segk_ref, o_ref, lse_ref):
    half = (pl.program_id(1) // per_kv) % 2
    length = k_ref.shape[0]
    k, v = doubled(k_ref[...], half), doubled(v_ref[...], half)
    low = lane_index((TILE, LANES)) < HEAD_SIZE
    q_at = lax.broadcasted_iota(jnp.int32, (TILE, TILE), 0)
    k_at = lax.broadcasted_iota(jnp.int32, (TILE, TILE), 1)
    for i in range(length // TILE):
        rows = slice(i * TILE, (i + 1) * TILE)
        reach = (i + 1) * TILE
        q = q_ref[rows, :]
        same = segq_ref[rows, :] == segk_ref[:, :reach]
        last = same[:, i * TILE :] & (k_at <= q_at)
        allowed = jnp.concatenate([same[:, : i * TILE], last], axis=1) if i else last
        outs = []
        for head in range(2):
            mine = jnp.where(low == (head == 0), q, jnp.zeros_like(q))
            raw = dot(mine, k[:reach], NT)
            scores = jnp.where(allowed, MULTIPLIER * raw, MASK_VALUE)
            top = jnp.max(scores, axis=1, keepdims=True)
            e = jnp.exp(scores - top)
            total = jnp.sum(e, axis=1, keepdims=True)
            p = (e * (1.0 / total)).astype(LOW)
            outs.append(dot(p, v[:reach]))
            lse = top + jnp.log(total)
            lse_ref[0, head : head + 1, rows] = jnp.transpose(
                jnp.broadcast_to(lse, (TILE, LANES))
            )[:1]
        o_ref[rows, :] = jnp.where(low, outs[0], outs[1]).astype(LOW)


def attend(qkv, q_width, kv_width, seg_col, seg_row, seqs):
    rows = qkv.shape[0]
    length = rows // seqs
    pairs, kv_pairs = q_width // LANES, kv_width // LANES
    per_kv = pairs // kv_pairs // 2
    return pl.pallas_call(
        functools.partial(attend_kernel, per_kv),
        grid=(seqs, pairs),
        in_specs=[
            pl.BlockSpec((length, LANES), lambda s, h: (s, h)),
            pl.BlockSpec((length, LANES), lambda s, h: (s, pairs + h // (2 * per_kv))),
            pl.BlockSpec((length, LANES), lambda s, h: (s, pairs + kv_pairs + h // (2 * per_kv))),
            pl.BlockSpec((length, 1), lambda s, h: (s, 0)),
            pl.BlockSpec((None, 1, length), lambda s, h: (s, 0, 0)),
        ],
        out_specs=[
            pl.BlockSpec((length, LANES), lambda s, h: (s, h)),
            pl.BlockSpec((1, 2, length), lambda s, h: (h, 0, s)),
        ],
        out_shape=[
            jax.ShapeDtypeStruct((rows, q_width), LOW),
            jax.ShapeDtypeStruct((pairs, 2, rows), WIDE),
        ],
        cost_estimate=COST,
        name="attend",
    )(qkv, qkv, qkv, seg_col, seg_row)


def attend_back_kernel(
    per_kv,
    q_ref,
    k_ref,
    v_ref,
    g_ref,
    lse_ref,
    segc_ref,
    segr_ref,
    cos_ref,
    sin_ref,
    out_ref,
    dk_acc,
    dv_acc,
    p_buf,
    dp_buf,
):
    pair, pairs = pl.program_id(1), pl.num_programs(1)
    slot = (pair // per_kv) % 2
    length = k_ref.shape[0]
    k, v = doubled(k_ref[...], slot), doubled(v_ref[...], slot)
    low = lane_index((TILE, LANES)) < HEAD_SIZE
    k_at = lax.broadcasted_iota(jnp.int32, (TILE, TILE), 0)
    q_at = lax.broadcasted_iota(jnp.int32, (TILE, TILE), 1)

    @pl.when(pair % per_kv == 0)
    def _():
        dk_acc[slot] = jnp.zeros_like(dk_acc[slot])
        dv_acc[slot] = jnp.zeros_like(dv_acc[slot])

    for i in range(length // TILE):
        rows = slice(i * TILE, (i + 1) * TILE)
        q, g = q_ref[rows, :], g_ref[rows, :]
        dq = []
        for head in range(2):
            chosen = low == (head == 0)
            qh = jnp.where(chosen, q, jnp.zeros_like(q))
            gh = jnp.where(chosen, g, jnp.zeros_like(g))
            lse = lse_ref[0, head : head + 1, rows]
            inner = jnp.zeros((1, TILE), WIDE)
            for j in range(i + 1):
                keys = slice(j * TILE, (j + 1) * TILE)
                allowed = segc_ref[keys, :] == segr_ref[:, rows]
                if i == j:
                    allowed = allowed & (k_at <= q_at)
                raw = dot(k[keys], qh, NT)
                p = jnp.exp(jnp.where(allowed, MULTIPLIER * raw, MASK_VALUE) - lse)
                dp = dot(v[keys], gh, NT)
                inner = inner + jnp.sum(p * dp, axis=0, keepdims=True)
                p_buf[keys, :] = p
                dp_buf[keys, :] = dp
            total = jnp.zeros((TILE, LANES), WIDE)
            for j in range(i + 1):
                keys = slice(j * TILE, (j + 1) * TILE)
                p = p_buf[keys, :]
                ds = (p * (dp_buf[keys, :] - inner)).astype(LOW)
                dv_acc[slot, keys, :] += dot(p.astype(LOW), gh)
                dk_acc[slot, keys, :] += dot(ds, qh)
                total = total + dot(ds, k[keys], TN)
            dq.append(total)
        out_ref[rows, pl.ds(pl.multiple_of(pair * LANES, LANES), LANES)] = turn(
            MULTIPLIER * jnp.where(low, dq[0], dq[1]), cos_ref[rows, :], -sin_ref[rows, :]
        ).astype(LOW)

    @pl.when(pair % (2 * per_kv) == 2 * per_kv - 1)
    def _():
        low_all = lane_index((length, LANES)) < HEAD_SIZE

        def folded(acc):
            a, b = acc[0], acc[1]
            a = a + pltpu.roll(a, HEAD_SIZE, 1)
            b = b + pltpu.roll(b, HEAD_SIZE, 1)
            return jnp.where(low_all, a, b)

        kv_pair = pair // (2 * per_kv)
        key_at = pl.multiple_of((pairs + kv_pair) * LANES, LANES)
        value_at = pl.multiple_of((pairs + pairs // (2 * per_kv) + kv_pair) * LANES, LANES)
        out_ref[:, pl.ds(key_at, LANES)] = turn(
            MULTIPLIER * folded(dk_acc), cos_ref[...], -sin_ref[...]
        ).astype(LOW)
        out_ref[:, pl.ds(value_at, LANES)] = folded(dv_acc).astype(LOW)


def attend_back(qkv, q_width, kv_width, g, lse, seg_col, seg_row, cosine, sine, seqs):
    rows = qkv.shape[0]
    length = rows // seqs
    pairs, kv_pairs = q_width // LANES, kv_width // LANES
    per_kv = pairs // kv_pairs // 2
    by_pair = lambda s, h: (s, h)
    by_seq = lambda s, h: (s, 0)
    return pl.pallas_call(
        functools.partial(attend_back_kernel, per_kv),
        grid=(seqs, pairs),
        in_specs=[
            pl.BlockSpec((length, LANES), by_pair),
            pl.BlockSpec((length, LANES), lambda s, h: (s, pairs + h // (2 * per_kv))),
            pl.BlockSpec((length, LANES), lambda s, h: (s, pairs + kv_pairs + h // (2 * per_kv))),
            pl.BlockSpec((length, LANES), by_pair),
            pl.BlockSpec((1, 2, length), lambda s, h: (h, 0, s)),
            pl.BlockSpec((length, 1), by_seq),
            pl.BlockSpec((None, 1, length), lambda s, h: (s, 0, 0)),
            pl.BlockSpec((length, LANES), by_seq),
            pl.BlockSpec((length, LANES), by_seq),
        ],
        out_specs=pl.BlockSpec((length, qkv.shape[1]), by_seq),
        out_shape=jax.ShapeDtypeStruct(qkv.shape, LOW),
        scratch_shapes=[
            pltpu.VMEM((2, length, LANES), WIDE),
            pltpu.VMEM((2, length, LANES), WIDE),
            pltpu.VMEM((length, TILE), WIDE),
            pltpu.VMEM((length, TILE), WIDE),
        ],
        cost_estimate=COST,
        name="attend_back",
    )(qkv, qkv, qkv, g, lse, seg_col, seg_row, cosine, sine)


def branch_kernel(count, at_ref, *refs):
    w_ref, out_ref, held, sems = refs[count:]

    @pl.when(pl.program_id(0) == 0)
    def _():
        load_shares(refs[:count], held, sems)

    out_ref[...] = dot(held[...], w_ref[...], NT)


def branch(shares, w_down, at):
    count, width, rows = len(shares), shares[0].shape[1], rows_in(shares)
    units = w_down.shape[0] // 2
    tiles = units // TILE
    return pl.pallas_call(
        functools.partial(branch_kernel, count),
        grid_spec=pltpu.PrefetchScalarGridSpec(
            num_scalar_prefetch=1,
            grid=(tiles,),
            in_specs=[pl.BlockSpec(memory_space=pl.ANY)] * count
            + [pl.BlockSpec((TILE, width), lambda i, at: (at[0] * tiles + i, 0))],
            out_specs=pl.BlockSpec((rows, TILE), lambda i, at: (0, i)),
            scratch_shapes=[
                pltpu.VMEM((rows, width), LOW),
                pltpu.SemaphoreType.DMA((count,)),
            ],
        ),
        out_shape=jax.ShapeDtypeStruct((rows, units), WIDE),
        cost_estimate=COST,
        name="branch",
    )(at, *shares, w_down)


def mix_kernel(count, at_ref, *refs):
    share_refs, (wg_ref, wu_ref, dm_ref) = refs[:count], refs[count : count + 3]
    m_ref, dg_ref, du_ref, held, sems = refs[-5:]

    @pl.when(pl.program_id(0) == 0)
    def _():
        load_shares(share_refs, held, sems)

    n = held[...]
    g = dot(n, wg_ref[...])
    u = dot(n, wu_ref[...])
    dm = dm_ref[...]
    s = jax.nn.sigmoid(g)
    active = g * s
    m_ref[...] = (active * u).astype(LOW)
    dg_ref[...] = (dm * u * s * (1.0 + g * (1.0 - s))).astype(LOW)
    du_ref[...] = (dm * active).astype(LOW)


def mix(shares, wg, wu, dm, at, block, given=()):
    count, width, rows = len(shares), shares[0].shape[1], rows_in(shares)
    tiles = dm.shape[1] // TILE
    weight = pl.BlockSpec((width, TILE), lambda i, at: (0, at[0] * tiles + i))
    spec = pl.BlockSpec((rows, TILE), lambda i, at: (block, i))
    return pl.pallas_call(
        functools.partial(mix_kernel, count),
        grid_spec=pltpu.PrefetchScalarGridSpec(
            num_scalar_prefetch=1,
            grid=(tiles,),
            in_specs=[pl.BlockSpec(memory_space=pl.ANY)] * count
            + [weight, weight, spec]
            + [pl.BlockSpec(memory_space=pl.ANY)] * len(given),
            out_specs=[spec] * 3,
            scratch_shapes=[
                pltpu.VMEM((rows, width), LOW),
                pltpu.SemaphoreType.DMA((count,)),
            ],
        ),
        out_shape=[jax.ShapeDtypeStruct(dm.shape, LOW)] * 3,
        input_output_aliases={count + 4 + i: i for i in range(len(given))},
        cost_estimate=COST,
        name="mix",
    )(at, *shares, wg, wu, dm, *given)


def unmix_kernel(at_ref, dg_ref, du_ref, wg_ref, wu_ref, *out_refs):
    total = dot(dg_ref[...], wg_ref[...], NT) + dot(du_ref[...], wu_ref[...], NT)
    share = out_refs[0].shape[0]
    for i, ref in enumerate(out_refs):
        ref[...] = total[i * share : (i + 1) * share].astype(LOW)


def unmix(dg, du, wg, wu, at, block, share, pieces):
    units, width = dg.shape[1], wg.shape[0]
    rows = share * pieces
    given = pl.BlockSpec((rows, units), lambda i, at: (block, 0))
    moving = pl.BlockSpec((TILE, units), lambda i, at: (i, at[0]))
    return pl.pallas_call(
        unmix_kernel,
        grid_spec=pltpu.PrefetchScalarGridSpec(
            num_scalar_prefetch=1,
            grid=(width // TILE,),
            in_specs=[given, given, moving, moving],
            out_specs=[pl.BlockSpec((share, TILE), lambda i, at: (0, i))] * pieces,
        ),
        out_shape=[jax.ShapeDtypeStruct((share, width), LOW)] * pieces,
        cost_estimate=COST,
        name="unmix",
    )(at, dg, du, wg, wu)


def down_kernel(at_ref, m_ref, w_ref, *out_refs):
    total = dot(m_ref[...], w_ref[...])
    share = out_refs[0].shape[0]
    for i, ref in enumerate(out_refs):
        ref[...] = total[i * share : (i + 1) * share].astype(LOW)


def down(m, w_down, at, share):
    rows, units = m.shape
    width = w_down.shape[1]
    pieces = rows // share
    return pl.pallas_call(
        down_kernel,
        grid_spec=pltpu.PrefetchScalarGridSpec(
            num_scalar_prefetch=1,
            grid=(width // TILE,),
            in_specs=[
                pl.BlockSpec((rows, units), lambda i, at: (0, 0)),
                pl.BlockSpec((units, TILE), lambda i, at: (at[0], i)),
            ],
            out_specs=[pl.BlockSpec((share, TILE), lambda i, at: (0, i))] * pieces,
        ),
        out_shape=[jax.ShapeDtypeStruct((share, width), LOW)] * pieces,
        cost_estimate=COST,
        name="down",
    )(at, m, w_down)


def spread_kernel(count, columns_ref, rows_ref, *refs):
    out_ref = refs[-1]
    share = refs[0].shape[0]
    for i in range(count):
        out_ref[pl.ds(pl.multiple_of(rows_ref[i] * share, share), share), :] = refs[i][...]


def spread(shares, rows, block, masks, place, given=None, order=None):
    count, (share, width) = len(shares), shares[0].shape
    blocks = jnp.array(block_order(masks), jnp.int32) ^ place
    order = jnp.arange(count, dtype=jnp.int32) if order is None else order
    columns = width // (1 << len(masks))
    if columns % LANES:
        whole = jnp.zeros((rows, width), LOW) if given is None else given
        for i, a in enumerate(shares):
            piece = permute_columns(a, masks, place)
            first = (block * count + order[i]) * share
            whole = lax.dynamic_update_slice_in_dim(whole, piece, first, 0)
        return whole
    extra = [] if given is None else [given]
    return pl.pallas_call(
        functools.partial(spread_kernel, count),
        grid_spec=pltpu.PrefetchScalarGridSpec(
            num_scalar_prefetch=2,
            grid=(width // columns,),
            in_specs=[pl.BlockSpec((share, columns), lambda i, blocks, order: (0, blocks[i]))] * count
            + [pl.BlockSpec(memory_space=pl.ANY)] * len(extra),
            out_specs=pl.BlockSpec((count * share, columns), lambda i, blocks, order: (block, i)),
        ),
        out_shape=jax.ShapeDtypeStruct((rows, width), LOW),
        input_output_aliases={count + 2: 0} if extra else {},
        cost_estimate=COST,
        name="spread",
    )(blocks, order, *shares, *extra)


def product_rows(left, right, given, low, size, width, kind):
    tokens, across = right.shape
    tile = min(TILE, size * width)
    tiles = size * width // tile

    def kernel(left_ref, right_ref, *refs):
        value = dot(left_ref[...], right_ref[...], TN)
        for ref in refs[:-1]:
            value = value + ref[...].astype(WIDE)
        refs[-1][...] = value.astype(kind)

    def at(first):
        start = (low - first) * width // tile
        return lambda i: (start + i, 0)

    start = low * width // tile
    return pl.pallas_call(
        kernel,
        grid=(tiles,),
        in_specs=[
            pl.BlockSpec((tokens, tile), lambda i: (0, start + i)),
            pl.BlockSpec((tokens, across), lambda i: (0, 0)),
        ]
        + [pl.BlockSpec((tile, across), at(first)) for first, _ in given],
        out_specs=pl.BlockSpec((tile, across), lambda i: (i, 0)),
        out_shape=jax.ShapeDtypeStruct((size * width, across), kind),
        cost_estimate=COST,
        name="product_rows",
    )(left, right, *(array for _, array in given))


def product_cols(left, right, given, low, size, width, kind):
    tokens, down_to = left.shape
    across = size * width
    tile = min(TILE, down_to)

    def kernel(left_ref, right_ref, *refs):
        value = dot(left_ref[...], right_ref[...], TN)
        for ref in refs[:-1]:
            value = value + ref[...].astype(WIDE)
        refs[-1][...] = value.astype(kind)

    def at(first):
        start = (low - first) // size
        return lambda i: (i, start)

    return pl.pallas_call(
        kernel,
        grid=(down_to // tile,),
        in_specs=[
            pl.BlockSpec((tokens, tile), lambda i: (0, i)),
            pl.BlockSpec((tokens, across), lambda i: (0, low // size)),
        ]
        + [pl.BlockSpec((tile, across), at(first)) for first, _ in given],
        out_specs=pl.BlockSpec((tile, across), lambda i: (i, 0)),
        out_shape=jax.ShapeDtypeStruct((down_to, across), kind),
        cost_estimate=COST,
        name="product_cols",
    )(left, right, *(array for _, array in given))


def half_kernel(axis, at_ref, own_ref, other_ref, out_ref):
    size = own_ref.shape[axis]
    for ref, half in ((own_ref, at_ref[0]), (other_ref, 1 - at_ref[0])):
        where = pl.ds(pl.multiple_of(half * size, size), size)
        if axis == 0:
            out_ref[where, :] = ref[...].astype(WIDE)
        else:
            out_ref[:, where] = ref[...].astype(WIDE)


def halves(own, other, at, axis):
    shape = list(own.shape)
    shape[axis] *= 2
    return pl.pallas_call(
        functools.partial(half_kernel, axis),
        grid_spec=pltpu.PrefetchScalarGridSpec(
            num_scalar_prefetch=1,
            grid=(1,),
            in_specs=[pl.BlockSpec(own.shape, lambda i, at: (0, 0))] * 2,
            out_specs=pl.BlockSpec(tuple(shape), lambda i, at: (0, 0)),
        ),
        out_shape=jax.ShapeDtypeStruct(tuple(shape), WIDE),
        cost_estimate=COST,
        name="halves",
    )(at, own, other)


def whole(function, shapes, *arrays):
    def kernel(*refs):
        results = function(*(ref[...] for ref in refs[: len(arrays)]))
        for ref, value in zip(refs[len(arrays) :], results):
            ref[...] = value.astype(ref.dtype)

    return pl.pallas_call(
        kernel,
        out_shape=[jax.ShapeDtypeStruct(shape, kind) for shape, kind in shapes],
        in_specs=[pl.BlockSpec(memory_space=pltpu.VMEM)] * len(arrays),
        out_specs=[pl.BlockSpec(memory_space=pltpu.VMEM)] * len(shapes),
        cost_estimate=COST,
        name="whole",
    )(*arrays)


def norm_back_kernel(count, d_ref, value_ref, inverse_ref, gain_ref, *refs):
    term_refs, (dx_ref, low_ref, gain_out_ref) = refs[:count], refs[count:]
    d_normed = term_refs[0][...].astype(WIDE)
    for ref in term_refs[1:]:
        d_normed = d_normed + ref[...].astype(WIDE)
    values, inverse = value_ref[...].astype(WIDE), inverse_ref[...]
    scaled = d_normed * gain_ref[...].astype(WIDE)
    mean = jnp.mean(scaled * values, axis=-1, keepdims=True)
    dx = d_ref[...].astype(WIDE) + inverse * scaled - values * (inverse * inverse * inverse * mean)
    dx_ref[...] = dx.astype(dx_ref.dtype)
    low_ref[...] = (RESIDUAL_SCALE * dx).astype(LOW)

    @pl.when(pl.program_id(0) == 0)
    def _():
        gain_out_ref[...] = jnp.zeros_like(gain_out_ref)

    gain_out_ref[...] += jnp.sum(d_normed * values * inverse, axis=0, keepdims=True)


def norm_back(d_rows, values, inverse, gain, terms, kind, tile=64):
    rows, width = values.shape
    spec = pl.BlockSpec((tile, width), lambda i: (i, 0))
    fixed = pl.BlockSpec((1, width), lambda i: (0, 0))
    return pl.pallas_call(
        functools.partial(norm_back_kernel, len(terms)),
        grid=(rows // tile,),
        in_specs=[spec, spec, pl.BlockSpec((tile, 1), lambda i: (i, 0)), fixed] + [spec] * len(terms),
        out_specs=[spec, spec, fixed],
        out_shape=[
            jax.ShapeDtypeStruct((rows, width), kind),
            jax.ShapeDtypeStruct((rows, width), LOW),
            jax.ShapeDtypeStruct((1, width), WIDE),
        ],
        cost_estimate=COST,
        name="norm_back",
    )(d_rows, values, inverse, gain.reshape(1, -1), *terms)


def sum_all_kernel(steps, part_ref, out_ref, sent, got, send_sems, got_sems):
    partners = []
    for axis, mask in steps:
        mine = lax.axis_index(axis)
        partners.append({axis: mine + mask * (1 - 2 * (mine // mask % 2))})
    barrier = pltpu.get_barrier_semaphore()
    for partner in partners:
        pl.semaphore_signal(barrier, inc=1, device_id=partner, device_id_type=pl.DeviceIdType.MESH)
    pl.semaphore_wait(barrier, len(partners))
    total = part_ref[...]
    for i, partner in enumerate(partners):
        sent[i] = total
        copy = pltpu.make_async_remote_copy(
            src_ref=sent.at[i],
            dst_ref=got.at[i],
            send_sem=send_sems.at[i],
            recv_sem=got_sems.at[i],
            device_id=partner,
            device_id_type=pl.DeviceIdType.MESH,
        )
        copy.start()
        copy.wait()
        total = total + got[i]
    out_ref[...] = total


def sum_all(part, steps):
    count = len(steps)
    return pl.pallas_call(
        functools.partial(sum_all_kernel, steps),
        out_shape=jax.ShapeDtypeStruct(part.shape, part.dtype),
        in_specs=[pl.BlockSpec(memory_space=pltpu.VMEM)],
        out_specs=pl.BlockSpec(memory_space=pltpu.VMEM),
        scratch_shapes=[
            pltpu.VMEM((count, *part.shape), part.dtype),
            pltpu.VMEM((count, *part.shape), part.dtype),
            pltpu.SemaphoreType.DMA((count,)),
            pltpu.SemaphoreType.DMA((count,)),
        ],
        compiler_params=pltpu.CompilerParams(collective_id=0, has_side_effects=True),
        cost_estimate=COST,
        name="sum_all",
    )(part)


NEAR, FAR, PAIR = 1, 2, 2


def swap(array, axis, mask):
    size = lax.axis_size(axis)
    return lax.ppermute(array, axis, [(i, i ^ mask) for i in range(size)])


def powers(size):
    return [1 << i for i in range(size.bit_length() - 1)]


def swap_both(array):
    count = lax.axis_size("tensor")
    size = lax.axis_size("dp") * count
    mask = PAIR * count + FAR
    return lax.ppermute(array, ("dp", "tensor"), [(i, i ^ mask) for i in range(size)])


def cut(array):
    half = array.shape[0] // 2
    return array[:half], array[half:]


def added(*arrays):
    total = arrays[0].astype(WIDE)
    for a in arrays[1:]:
        total = total + a.astype(WIDE)
    return total


def add_low(*arrays):
    return whole(lambda *a: (added(*a),), [(arrays[0].shape, LOW)], *arrays)[0]


def joined(mine, got):
    rows, width = mine.shape
    return whole(lambda a, b: cut(added(a, b)), [((rows // 2, width), LOW)] * 2, mine, got)


class GroupSum:
    def near(self, *chips):
        return [swap(chip[1], "tensor", NEAR) for chip in chips]

    def start_both(self, lane, both):
        (got,) = self.near(both)
        low, high = lane(joined, both[0], got)
        self.low, self.high = swap(low, "tensor", FAR), swap(high, "dp", PAIR)

    def start_far_pair(self, lane, own, far, pair):
        got_own, got_far, got_pair = self.near(own, far, pair)

        def relay(own, got_own, far, got_far, high, pair, got_pair, low):
            far, pair = added(far, got_far), added(pair, got_pair)
            rows = low.shape[0]
            far = jnp.concatenate([far[:rows], far[rows:] + high.astype(WIDE)], axis=0)
            pair = jnp.concatenate([pair[:rows] + low.astype(WIDE), pair[rows:]], axis=0)
            return added(own, got_own), far, pair

        self.own, far, pair = lane(
            functools.partial(whole, relay, [(own[0].shape, kind) for kind in (WIDE, LOW, LOW)]),
            own[0],
            got_own,
            far[0],
            got_far,
            self.high,
            pair[0],
            got_pair,
            self.low,
        )
        self.far, self.pair = swap(far, "tensor", FAR), swap(pair, "dp", PAIR)

    def terms(self):
        return self.own, self.far, self.pair


def block_order(masks):
    order = [0]
    for mask in reversed(masks):
        order = [mask ^ b for b in order] + order
    return order


def permute_columns(array, masks, place):
    count = 1 << len(masks)
    width = array.shape[1] // count
    return jnp.concatenate(
        [
            lax.dynamic_slice_in_dim(array, (place ^ b) * width, width, 1)
            for b in block_order(masks)
        ],
        axis=1,
    )


class Reduction:
    def __init__(self, left, right, masks, axis):
        self.left, self.right, self.masks, self.axis = left, right, list(masks), axis
        self.count = 1 << len(masks)
        self.width = (right if axis else left).shape[1] // self.count
        self.low, self.size, self.got = 0, self.count // 2, []

    def total(self, lane, low, high):
        firsts = [first for first, _ in self.got]
        width, axis = self.width, self.axis
        kind = WIDE if high == self.count else LOW

        def compute(left, right, *arrays):
            if (high - low) * width % LANES == 0:
                product = product_cols if axis else product_rows
                return product(left, right, list(zip(firsts, arrays)), low, high - low, width, kind)
            part = slice(low * width, high * width)
            value = dot(left, right[:, part], TN) if axis else dot(left[:, part], right, TN)
            for first, array in zip(firsts, arrays):
                piece = lax.slice_in_dim(
                    array, (low - first) * width, (high - first) * width, axis=axis
                )
                value = value + piece.astype(WIDE)
            return value.astype(kind)

        return lane(compute, self.left, self.right, *(array for _, array in self.got))

    def step(self, lane):
        sent = self.total(lane, self.low, self.low + self.size)
        self.low += self.size
        self.size //= 2
        self.got.append((self.low, swap(sent, "dp", self.masks.pop(0))))
        return self

    def finish(self, lane):
        while self.masks:
            self.step(lane)
        return self.total(lane, self.low, self.count)

    def step_half(self, lane):
        while len(self.masks) > 1:
            self.step(lane)
        sent = self.total(lane, self.low, self.low + self.size)
        self.low += self.size
        self.other = swap(sent, "dp", self.masks.pop(0))
        return self

    def finish_half(self, lane, at):
        own = self.total(lane, self.low, self.count)
        return lane(lambda a, b, at: halves(a, b, at, 1 - self.axis), own, self.other, at)


def rows_of(shares):
    return jnp.concatenate(shares, axis=0)


def inverse_rms(value_rows):
    return lax.rsqrt(jnp.mean(value_rows * value_rows, axis=-1, keepdims=True) + EPSILON)


def body(
    layer_in,
    cotangent,
    segments,
    gain_attn,
    w_query,
    key_weight,
    value_weight,
    w_out,
    gain_ffn,
    w_gate,
    w_up,
    w_down,
):
    share, width = layer_in.shape
    count = lax.axis_size("tensor")
    rank = lax.axis_index("tensor")
    place = lax.axis_index("dp")
    masks = powers(lax.axis_size("dp"))
    group_masks = [m for m in masks if m != PAIR] + [PAIR]
    at = place // PAIR % 2
    at_array = at.reshape(1).astype(jnp.int32)
    order = jnp.arange(count, dtype=jnp.int32) ^ rank
    seqs = segments.shape[0]
    q_width, kv_width = w_query.shape[1], key_weight.shape[1]
    rows = count * share
    lane = Lane()


    def first_norm(layer_in, gain):
        x = layer_in.astype(WIDE)
        inverse = inverse_rms(x)
        return (x * inverse * gain.astype(WIDE)).astype(LOW), inverse

    n1_own, inverse_one = lane(first_norm, layer_in, gain_attn)
    n1_far, n1_near = swap(n1_own, "tensor", FAR), swap(n1_own, "tensor", NEAR)

    def prepare(segments, w_query, key_weight, value_weight, cotangent):
        tables = rope_tables(positions_of(segments).reshape(-1))
        w_qkv = jnp.concatenate([w_query, key_weight, value_weight], axis=1)
        seg_col, seg_row = segments.reshape(-1, 1), segments[:, None, :]
        branch_own = (RESIDUAL_SCALE * cotangent.astype(WIDE)).astype(LOW)
        return tables, w_qkv, seg_col, seg_row, branch_own

    tables, w_qkv, seg_col, seg_row, branch_own = lane(
        prepare, segments, w_query, key_weight, value_weight, cotangent
    )
    turned = q_width + kv_width
    qkv = lane(
        lambda a, b, order, w, c, s: project([a, b], order, w, rows, NN, turned, (c, s)),
        n1_own,
        n1_near,
        order[:2],
        w_qkv,
        *tables,
    )
    n1_other = swap(n1_far, "tensor", NEAR)
    branch_own = after(branch_own, n1_far)
    branch_chips = [
        branch_own,
        swap_both(branch_own),
        swap(branch_own, "tensor", FAR),
        swap(branch_own, "dp", PAIR),
    ]
    qkv = lane(
        lambda a, b, order, w, c, s, q: project([a, b], order, w, rows, NN, turned, (c, s), (q,)),
        n1_far,
        n1_other,
        order[2:],
        w_qkv,
        *tables,
        qkv,
    )
    attended, lse = lane(
        lambda q, c, r: attend(q, q_width, kv_width, c, r, seqs), qkv, seg_col, seg_row
    )
    parts = lane(lambda a, w, o: pieces(a, w, o, count, False), attended, w_out, order)
    got_near, got_other = swap(parts[1], "tensor", NEAR), swap(parts[3], "tensor", NEAR)
    sent = lane(lambda a, b: added(a, b).astype(LOW), parts[2], got_other)
    got_far = swap(sent, "tensor", FAR)

    branch_shares = [b for a in branch_chips for b in (a, swap(a, "tensor", NEAR))]
    d_mixed = lane(lambda a, w, at: branch(a, w, at), branch_shares, w_down, at_array)
    branch_spread = lane(lambda a: spread(a, 2 * rows, 0, group_masks, place), branch_shares)

    def second_norm(layer_in, mine, near, far, gain):
        hidden = layer_in.astype(WIDE) + RESIDUAL_SCALE * added(mine, near, far)
        inverse = inverse_rms(hidden)
        return hidden, inverse, (hidden * inverse * gain.astype(WIDE)).astype(LOW)

    hidden, inverse_two, n2_own = lane(
        second_norm, layer_in, parts[0], got_near, got_far, gain_ffn
    )
    n2_far, n2_pair = swap(n2_own, "tensor", FAR), swap(n2_own, "dp", PAIR)
    n2_own = [n2_own, swap(n2_own, "tensor", NEAR)]
    blend = lambda block: lambda a, g, u, d, at, *m: mix(a, g, u, d, at, block, m)
    scatter = lambda block: lambda a, *n: spread(a, 2 * rows, block, group_masks, place, *n)
    mixed = lane(blend(0), n2_own, w_gate, w_up, d_mixed, at_array)
    n2 = lane(scatter(0), n2_own)
    n2_far, n2_pair = after((n2_far, n2_pair), n2)
    n2_both = [swap(cut(n2_pair)[0], "tensor", FAR), swap(cut(n2_far)[1], "dp", PAIR)]
    n2_four = [n2_far, swap(n2_far, "tensor", NEAR), n2_pair, swap(n2_pair, "tensor", NEAR)]
    mixed = lane(blend(1), n2_four, w_gate, w_up, d_mixed, at_array, *mixed)
    n2 = lane(scatter(1), n2_four, n2)
    n2_both = n2_both + [swap(a, "tensor", NEAR) for a in n2_both]
    mixed, d_gate, d_upper = lane(blend(1), n2_both, w_gate, w_up, d_mixed, at_array, *mixed)

    grad_down = Reduction(mixed, branch_spread, group_masks, 1).step(lane)
    back = lambda block, pieces: lambda dg, du, wg, wu, at: unmix(
        dg, du, wg, wu, at, block, share, pieces
    )
    ffn = (d_gate, d_upper, w_gate, w_up, at_array)
    d_normed = GroupSum()
    dn_both = lane(back(1, 2), *ffn)
    dn_four = lane(back(1, 4), *ffn)
    d_normed.start_both(lane, dn_both)
    dn_own = lane(back(0, 2), *ffn)
    n2 = lane(
        lambda a, n: spread(a, 2 * rows, 1, group_masks, place, n), n2_both, n2
    )
    d_normed.start_far_pair(lane, dn_own, dn_four[:2], dn_four[2:])
    grad_gate = Reduction(n2, d_gate, group_masks, 0).step(lane)
    grad_down.step(lane)
    grad_up = Reduction(n2, d_upper, group_masks, 0).step(lane)
    ffn_parts = lane(lambda m, w, at: down(m, w, at, share), mixed, w_down, at_array)
    d_hidden, da_own, gain_two_part = lane(
        lambda c, h, i, g, *t: norm_back(c, h, i, g, t, WIDE),
        cotangent,
        hidden,
        inverse_two,
        gain_ffn,
        *d_normed.terms(),
    )
    da_far, da_near = swap(da_own, "tensor", FAR), swap(da_own, "tensor", NEAR)
    n1_shares = [n1_own, n1_near, n1_far, n1_other]
    natural = lambda a, o: spread(a, rows, 0, masks, place, None, o)
    n1 = lane(natural, n1_shares, order)
    grad_gate.step(lane)
    grad_down.step_half(lane)
    out_total = GroupSum()
    out_total.start_both(lane, ffn_parts[2:4])
    d_attn = lane(
        lambda a, b, o, w: project([a, b], o, w, rows, NT), da_own, da_near, order[:2], w_out
    )
    da_other = swap(after(da_far, d_attn), "tensor", NEAR)
    d_attn = lane(
        lambda a, b, o, w, d: project([a, b], o, w, rows, NT, given=(d,)),
        da_far,
        da_other,
        order[2:],
        w_out,
        d_attn,
    )
    out_total.start_far_pair(lane, ffn_parts[:2], ffn_parts[4:6], ffn_parts[6:8])

    d_qkv = lane(
        lambda q, g, l, c, r, a, b: attend_back(q, q_width, kv_width, g, l, c, r, a, b, seqs),
        qkv,
        d_attn,
        lse,
        seg_col,
        seg_row,
        *tables,
    )
    grad_gate.step_half(lane)
    out_rows = lane(
        lambda hidden, *terms: whole(
            lambda hidden, *terms: (hidden + RESIDUAL_SCALE * added(*terms),),
            [(hidden.shape, LOW)],
            hidden,
            *terms,
        )[0],
        hidden,
        *out_total.terms(),
    )
    parts = lane(lambda a, w, o: pieces(a, w, o, count, True), d_qkv, w_qkv, order)
    got_near, got_other = swap(parts[1], "tensor", NEAR), swap(parts[3], "tensor", NEAR)
    grad_qkv = Reduction(n1, d_qkv, masks, 0).step(lane)
    kept, sent = lane(
        lambda *a: whole(
            lambda a, b, c, d: (added(a, b), added(c, d)),
            [(a[0].shape, WIDE), (a[0].shape, LOW)],
            *a,
        ),
        parts[0],
        got_near,
        parts[2],
        got_other,
    )
    got_far = swap(sent, "tensor", FAR)
    grad_up.step(lane)
    grad_down = grad_down.finish_half(lane, at_array)
    da = lane(natural, [da_own, da_near, da_far, da_other], order)
    grad_wout = Reduction(attended, da, masks, 1).step(lane)
    grad_rows, _, gain_one_part = lane(
        lambda c, h, i, g, *t: norm_back(c, h, i, g, t, LOW),
        d_hidden,
        layer_in,
        inverse_one,
        gain_attn,
        kept,
        got_far,
    )
    grad_gate = grad_gate.finish_half(lane, at_array)
    grad_qkv.step(lane)
    grad_up.step_half(lane)
    grad_wout.step(lane)
    grad_qkv.step(lane)
    grad_up = grad_up.finish_half(lane, at_array)
    grad_wout.step(lane)
    grad_qkv = grad_qkv.finish(lane)
    grad_wout = grad_wout.finish(lane)
    steps = [("tensor", m) for m in powers(count)] + [("dp", m) for m in masks]
    gains = lane(
        lambda a, b: sum_all(jnp.concatenate([a, b], axis=0), steps), gain_one_part, gain_two_part
    )
    block = width // lax.axis_size("dp")
    gains = lax.dynamic_slice_in_dim(gains, place * block, block, 1)
    return (
        out_rows,
        grad_rows,
        gains[0],
        grad_qkv[:, :q_width],
        grad_qkv[:, q_width : q_width + kv_width],
        grad_qkv[:, q_width + kv_width :],
        grad_wout,
        gains[1],
        grad_gate,
        grad_up,
        grad_down,
    )


def solution(mesh):
    return jax.shard_map(
        body,
        mesh=mesh,
        in_specs=(
            P(("dp", "tensor"), None),
            P(("dp", "tensor"), None),
            P("dp", None),
            P(),
            P(None, "tensor"),
            P(None, "tensor"),
            P(None, "tensor"),
            P("tensor", None),
            P(),
            P(None, "tensor"),
            P(None, "tensor"),
            P("tensor", None),
        ),
        out_specs=(
            P(("dp", "tensor"), None),
            P(("dp", "tensor"), None),
            P("dp"),
            P("dp", "tensor"),
            P("dp", "tensor"),
            P("dp", "tensor"),
            P("tensor", "dp"),
            P("dp"),
            P("dp", "tensor"),
            P("dp", "tensor"),
            P("tensor", "dp"),
        ),
        check_vma=False,
    )
```

```python
import functools

import jax
import jax.numpy as jnp
from jax import lax
from jax.experimental import pallas as pl
from jax.experimental.pallas import tpu as pltpu
from jax.sharding import PartitionSpec as P

HEAD_SIZE = 64


EPSILON = 1e-05
MULTIPLIER = 0.015625
RESIDUAL_SCALE = 0.22
THETA_BASE = 10000.0
MASK_VALUE = -1e30
LOW = jnp.bfloat16
WIDE = jnp.float32
LANES = 128
TILE = 256
WIDE_TILE = 512

NEAR, FAR, PAIR = 1, 2, 2
NN = (((1,), (0,)), ((), ()))
NT = (((1,), (1,)), ((), ()))
TN = (((0,), (0,)), ((), ()))
COST = pl.CostEstimate(flops=1, bytes_accessed=1, transcendentals=0)
IDS = {
    "sum_all": 0,
    "near_in": 1,
    "far_in": 2,
    "near_back": 3,
    "far_back": 4,
    "out_pieces": 5,
    "in_pieces": 6,
    "unmix": 7,
    "down": 8,
}


def dot(a, b, dims=NN):
    return lax.dot_general(a, b, dims, preferred_element_type=WIDE)


def after(value, *others):
    return lax.optimization_barrier((value, *others))[0]


class Lane:
    def __init__(self):
        self.last = ()

    def __call__(self, function, *operands):
        if self.last:
            operands = after(operands, *self.last)
        result = function(*operands)
        self.last = tuple(jax.tree.leaves(result))
        return result


def positions_of(seg_ids):
    length = seg_ids.shape[-1]
    index = jnp.broadcast_to(jnp.arange(length, dtype=jnp.int32), seg_ids.shape)
    before = jnp.concatenate([seg_ids[:, :1] - 1, seg_ids[:, :-1]], axis=1)
    starts = jnp.where(seg_ids != before, index, jnp.zeros_like(index))
    return index - lax.cummax(starts, axis=1)


def rope_tables(positions):
    half = HEAD_SIZE // 2
    freq = THETA_BASE ** (-2.0 * jnp.arange(half, dtype=jnp.float32) / HEAD_SIZE)
    angle = positions.astype(jnp.float32)[:, None] * freq[None, :]
    cosine, sine = jnp.cos(angle), jnp.sin(angle)
    repeats = LANES // HEAD_SIZE
    return (
        jnp.concatenate([cosine, cosine] * repeats, axis=1),
        jnp.concatenate([-sine, sine] * repeats, axis=1),
    )


def lane_index(shape):
    return lax.broadcasted_iota(jnp.int32, shape, len(shape) - 1)


def turn(u, cosine, sine):
    quarter = HEAD_SIZE // 2
    first = lane_index(u.shape) % HEAD_SIZE < quarter
    other = jnp.where(
        first, pltpu.roll(u, u.shape[1] - quarter, 1), pltpu.roll(u, quarter, 1)
    )
    return u * cosine + other * sine


def load_shares(share_refs, held, sems):
    copies, first = [], 0
    for i, ref in enumerate(share_refs):
        copies.append(pltpu.make_async_copy(ref, held.at[pl.ds(first, ref.shape[0])], sems.at[i]))
        first += ref.shape[0]
    for copy in copies:
        copy.start()
    for copy in copies:
        copy.wait()


def rows_in(shares):
    return sum(a.shape[0] for a in shares)


def near_core():
    mine = lax.axis_index("tensor")
    return {"tensor": mine + NEAR * (1 - 2 * (mine // NEAR % 2))}


def meet(partner):
    barrier = pltpu.get_barrier_semaphore()
    pl.semaphore_signal(barrier, inc=1, device_id=partner, device_id_type=pl.DeviceIdType.MESH)
    pl.semaphore_wait(barrier, 1)


def project_kernel(turned, dims, order_ref, share_ref, w_ref, *refs):
    tables = refs[:2]
    out_ref, other_ref, held, sems = refs[-4:]
    i, partner = pl.program_id(0), near_core()
    load = pltpu.make_async_copy(share_ref, held.at[0], sems.at[0])
    send = pltpu.make_async_remote_copy(
        src_ref=share_ref,
        dst_ref=other_ref,
        send_sem=sems.at[1],
        recv_sem=sems.at[2],
        device_id=partner,
        device_id_type=pl.DeviceIdType.MESH,
    )
    load_other = pltpu.make_async_copy(other_ref, held.at[1], sems.at[3])

    @pl.when(i == 0)
    def _():
        load.start()
        meet(partner)
        send.start()
        load.wait()

    @pl.when(i == 1)
    def _():
        send.wait()
        load_other.start()
        load_other.wait()

    out = dot(held[i], w_ref[...], dims)
    for j in range(out.shape[1] // LANES):
        part = out[:, j * LANES : (j + 1) * LANES]
        if j * LANES < turned:
            part = turn(part, tables[0][...], tables[1][...])
        out_ref[:, j * LANES : (j + 1) * LANES] = part.astype(LOW)


def project(own, order, weight, rows, dims, name, turned=0, tables=(), given=()):
    share, width = own.shape
    columns = weight.shape[1] if dims is NN else weight.shape[0]

    def moving(i, *_):
        mine = lax.axis_index("tensor")
        if "far" in name:
            mine = mine + FAR * (1 - 2 * (mine // FAR % 2))
        return mine + NEAR * (1 - 2 * (mine // NEAR % 2)) * i, 0

    return pl.pallas_call(
        functools.partial(project_kernel, turned, dims),
        grid_spec=pltpu.PrefetchScalarGridSpec(
            num_scalar_prefetch=1,
            grid=(2,),
            in_specs=[pl.BlockSpec(memory_space=pl.ANY)]
            + [pl.BlockSpec(weight.shape, lambda i, order: (0, 0))]
            + [pl.BlockSpec((share, LANES), moving)] * len(tables)
            + [pl.BlockSpec(memory_space=pl.ANY)] * len(given),
            out_specs=[pl.BlockSpec((share, columns), moving), pl.BlockSpec(memory_space=pl.ANY)],
            scratch_shapes=[
                pltpu.VMEM((2, share, width), LOW),
                pltpu.SemaphoreType.DMA((4,)),
            ],
        ),
        out_shape=[
            jax.ShapeDtypeStruct((rows, columns), LOW),
            jax.ShapeDtypeStruct(own.shape, LOW),
        ],
        input_output_aliases={3 + len(tables): 0} if given else {},
        compiler_params=pltpu.CompilerParams(collective_id=IDS[name], has_side_effects=True),
        cost_estimate=COST,
        name=name,
    )(order, own, weight, *tables, *given)


def paired_kernel(compute, count, share, *refs):
    half = count // 2
    got_refs, sent, send_sems, got_sems = refs[-3 - half : -3], *refs[-3:]
    mine_refs = refs[-3 - 2 * half : -3 - half]
    i, steps, partner = pl.program_id(0), pl.num_programs(0), near_core()
    tile = mine_refs[0].shape[1]

    def copy(step, k):
        columns = pl.ds(pl.multiple_of(step * tile, tile), tile)
        return pltpu.make_async_remote_copy(
            src_ref=sent.at[step % 2, k],
            dst_ref=got_refs[k].at[:, columns],
            send_sem=send_sems.at[step % 2, k],
            recv_sem=got_sems.at[step, k],
            device_id=partner,
            device_id_type=pl.DeviceIdType.MESH,
        )

    @pl.when(i == 0)
    def _():
        meet(partner)

    total = compute(refs[: -3 - 2 * half])
    for k in range(half):
        mine_refs[k][...] = total[2 * k * share : (2 * k + 1) * share].astype(LOW)

    @pl.when(i >= 2)
    def _():
        for k in range(half):
            copy(i - 2, k).wait_send()

    for k in range(half):
        sent[i % 2, k] = total[(2 * k + 1) * share : (2 * k + 2) * share].astype(LOW)

    @pl.when(i >= 1)
    def _():
        for k in range(half):
            copy(i - 1, k).start()

    @pl.when(i == steps - 1)
    def _():
        for k in range(half):
            copy(i, k).start()
        for k in range(half):
            copy(i - 1, k).wait_send()
            copy(i, k).wait_send()

        def arrived(step, carry):
            for k in range(half):
                copy(step, k).wait_recv()
            return carry

        lax.fori_loop(0, steps, arrived, 0)


def paired(compute, name, count, share, width, tile, in_specs, prefetch, *operands):
    half, steps = count // 2, width // tile
    piece = jax.ShapeDtypeStruct((share, width), LOW)
    results = pl.pallas_call(
        functools.partial(paired_kernel, compute, count, share),
        grid_spec=pltpu.PrefetchScalarGridSpec(
            num_scalar_prefetch=1,
            grid=(steps,),
            in_specs=in_specs,
            out_specs=[pl.BlockSpec((share, tile), lambda i, *_: (0, i))] * half
            + [pl.BlockSpec(memory_space=pl.ANY)] * half,
            scratch_shapes=[
                pltpu.VMEM((2, half, share, tile), LOW),
                pltpu.SemaphoreType.DMA((2, half)),
                pltpu.SemaphoreType.DMA((steps, half)),
            ],
        ),
        out_shape=[piece] * (2 * half),
        compiler_params=pltpu.CompilerParams(collective_id=IDS[name], has_side_effects=True),
        cost_estimate=COST,
        name=name,
    )(prefetch, *operands)
    return list(zip(results[:half], results[half:]))


def pieces(a, weight, order, count, dims, name):
    rows, depth = a.shape
    share = rows // count
    width = weight.shape[1] if dims is NN else weight.shape[0]
    tile = WIDE_TILE
    moving = (
        pl.BlockSpec((depth, tile), lambda i, *_: (0, i))
        if dims is NN
        else pl.BlockSpec((tile, depth), lambda i, *_: (i, 0))
    )

    def compute(refs):
        _, a_ref, w_ref = refs
        parts = []
        for i in range(count):
            block = lax.axis_index("tensor")
            for mask in powers(count):
                if i & mask:
                    block = block + mask * (1 - 2 * (block // mask % 2))
            parts.append(a_ref[pl.ds(pl.multiple_of(block * share, share), share), :])
        return dot(jnp.concatenate(parts, axis=0), w_ref[...], dims)

    given = pl.BlockSpec((rows, depth), lambda i, *_: (0, 0))
    return paired(compute, name, count, share, width, tile, [given, moving], order, a, weight)


def doubled(pair, half):
    swapped = pltpu.roll(pair.astype(WIDE), HEAD_SIZE, 1).astype(pair.dtype)
    low = lane_index(pair.shape) < HEAD_SIZE
    return jnp.where(low == (half == 0), pair, swapped)


def attend_kernel(per_kv, q_ref, k_ref, v_ref, segq_ref, segk_ref, o_ref, lse_ref):
    half = (pl.program_id(1) // per_kv) % 2
    length = k_ref.shape[0]
    k, v = doubled(k_ref[...], half), doubled(v_ref[...], half)
    low = lane_index((TILE, LANES)) < HEAD_SIZE
    q_at = lax.broadcasted_iota(jnp.int32, (TILE, TILE), 0)
    k_at = lax.broadcasted_iota(jnp.int32, (TILE, TILE), 1)
    for i in range(length // TILE):
        rows = slice(i * TILE, (i + 1) * TILE)
        reach = (i + 1) * TILE
        q = q_ref[rows, :]
        same = segq_ref[rows, :] == segk_ref[:, :reach]
        last = same[:, i * TILE :] & (k_at <= q_at)
        allowed = jnp.concatenate([same[:, : i * TILE], last], axis=1) if i else last
        outs = []
        for head in range(2):
            mine = jnp.where(low == (head == 0), q, jnp.zeros_like(q))
            raw = dot(mine, k[:reach], NT)
            scores = jnp.where(allowed, MULTIPLIER * raw, MASK_VALUE)
            top = jnp.max(scores, axis=1, keepdims=True)
            e = jnp.exp(scores - top)
            total = jnp.sum(e, axis=1, keepdims=True)
            p = (e * (1.0 / total)).astype(LOW)
            outs.append(dot(p, v[:reach]))
            lse = top + jnp.log(total)
            lse_ref[0, head : head + 1, rows] = jnp.transpose(
                jnp.broadcast_to(lse, (TILE, LANES))
            )[:1]
        o_ref[rows, :] = jnp.where(low, outs[0], outs[1]).astype(LOW)


def attend(qkv, q_width, kv_width, seg_col, seg_row, seqs):
    rows = qkv.shape[0]
    length = rows // seqs
    pairs, kv_pairs = q_width // LANES, kv_width // LANES
    per_kv = pairs // kv_pairs // 2
    return pl.pallas_call(
        functools.partial(attend_kernel, per_kv),
        grid=(seqs, pairs),
        in_specs=[
            pl.BlockSpec((length, LANES), lambda s, h: (s, h)),
            pl.BlockSpec((length, LANES), lambda s, h: (s, pairs + h // (2 * per_kv))),
            pl.BlockSpec((length, LANES), lambda s, h: (s, pairs + kv_pairs + h // (2 * per_kv))),
            pl.BlockSpec((length, 1), lambda s, h: (s, 0)),
            pl.BlockSpec((None, 1, length), lambda s, h: (s, 0, 0)),
        ],
        out_specs=[
            pl.BlockSpec((length, LANES), lambda s, h: (s, h)),
            pl.BlockSpec((1, 2, length), lambda s, h: (h, 0, s)),
        ],
        out_shape=[
            jax.ShapeDtypeStruct((rows, q_width), LOW),
            jax.ShapeDtypeStruct((pairs, 2, rows), WIDE),
        ],
        cost_estimate=COST,
        name="attend",
    )(qkv, qkv, qkv, seg_col, seg_row)


def attend_back_kernel(
    per_kv,
    q_ref,
    k_ref,
    v_ref,
    g_ref,
    lse_ref,
    segc_ref,
    segr_ref,
    cos_ref,
    sin_ref,
    out_ref,
    dk_acc,
    dv_acc,
    p_buf,
    dp_buf,
):
    pair, pairs = pl.program_id(1), pl.num_programs(1)
    slot = (pair // per_kv) % 2
    length = k_ref.shape[0]
    k, v = doubled(k_ref[...], slot), doubled(v_ref[...], slot)
    low = lane_index((TILE, LANES)) < HEAD_SIZE
    k_at = lax.broadcasted_iota(jnp.int32, (TILE, TILE), 0)
    q_at = lax.broadcasted_iota(jnp.int32, (TILE, TILE), 1)

    @pl.when(pair % per_kv == 0)
    def _():
        dk_acc[slot] = jnp.zeros_like(dk_acc[slot])
        dv_acc[slot] = jnp.zeros_like(dv_acc[slot])

    for i in range(length // TILE):
        rows = slice(i * TILE, (i + 1) * TILE)
        q, g = q_ref[rows, :], g_ref[rows, :]
        dq = []
        for head in range(2):
            chosen = low == (head == 0)
            qh = jnp.where(chosen, q, jnp.zeros_like(q))
            gh = jnp.where(chosen, g, jnp.zeros_like(g))
            lse = lse_ref[0, head : head + 1, rows]
            inner = jnp.zeros((1, TILE), WIDE)
            for j in range(i + 1):
                keys = slice(j * TILE, (j + 1) * TILE)
                allowed = segc_ref[keys, :] == segr_ref[:, rows]
                if i == j:
                    allowed = allowed & (k_at <= q_at)
                raw = dot(k[keys], qh, NT)
                p = jnp.exp(jnp.where(allowed, MULTIPLIER * raw, MASK_VALUE) - lse)
                dp = dot(v[keys], gh, NT)
                inner = inner + jnp.sum(p * dp, axis=0, keepdims=True)
                p_buf[keys, :] = p
                dp_buf[keys, :] = dp
            total = jnp.zeros((TILE, LANES), WIDE)
            for j in range(i + 1):
                keys = slice(j * TILE, (j + 1) * TILE)
                p = p_buf[keys, :]
                ds = (p * (dp_buf[keys, :] - inner)).astype(LOW)
                dv_acc[slot, keys, :] += dot(p.astype(LOW), gh)
                dk_acc[slot, keys, :] += dot(ds, qh)
                total = total + dot(ds, k[keys], TN)
            dq.append(total)
        out_ref[rows, pl.ds(pl.multiple_of(pair * LANES, LANES), LANES)] = turn(
            MULTIPLIER * jnp.where(low, dq[0], dq[1]), cos_ref[rows, :], -sin_ref[rows, :]
        ).astype(LOW)

    @pl.when(pair % (2 * per_kv) == 2 * per_kv - 1)
    def _():
        low_all = lane_index((length, LANES)) < HEAD_SIZE

        def folded(acc):
            a, b = acc[0], acc[1]
            a = a + pltpu.roll(a, HEAD_SIZE, 1)
            b = b + pltpu.roll(b, HEAD_SIZE, 1)
            return jnp.where(low_all, a, b)

        kv_pair = pair // (2 * per_kv)
        key_at = pl.multiple_of((pairs + kv_pair) * LANES, LANES)
        value_at = pl.multiple_of((pairs + pairs // (2 * per_kv) + kv_pair) * LANES, LANES)
        out_ref[:, pl.ds(key_at, LANES)] = turn(
            MULTIPLIER * folded(dk_acc), cos_ref[...], -sin_ref[...]
        ).astype(LOW)
        out_ref[:, pl.ds(value_at, LANES)] = folded(dv_acc).astype(LOW)


def attend_back(qkv, q_width, kv_width, g, lse, seg_col, seg_row, cosine, sine, seqs):
    rows = qkv.shape[0]
    length = rows // seqs
    pairs, kv_pairs = q_width // LANES, kv_width // LANES
    per_kv = pairs // kv_pairs // 2
    by_pair = lambda s, h: (s, h)
    by_seq = lambda s, h: (s, 0)
    return pl.pallas_call(
        functools.partial(attend_back_kernel, per_kv),
        grid=(seqs, pairs),
        in_specs=[
            pl.BlockSpec((length, LANES), by_pair),
            pl.BlockSpec((length, LANES), lambda s, h: (s, pairs + h // (2 * per_kv))),
            pl.BlockSpec((length, LANES), lambda s, h: (s, pairs + kv_pairs + h // (2 * per_kv))),
            pl.BlockSpec((length, LANES), by_pair),
            pl.BlockSpec((1, 2, length), lambda s, h: (h, 0, s)),
            pl.BlockSpec((length, 1), by_seq),
            pl.BlockSpec((None, 1, length), lambda s, h: (s, 0, 0)),
            pl.BlockSpec((length, LANES), by_seq),
            pl.BlockSpec((length, LANES), by_seq),
        ],
        out_specs=pl.BlockSpec((length, qkv.shape[1]), by_seq),
        out_shape=jax.ShapeDtypeStruct(qkv.shape, LOW),
        scratch_shapes=[
            pltpu.VMEM((2, length, LANES), WIDE),
            pltpu.VMEM((2, length, LANES), WIDE),
            pltpu.VMEM((length, TILE), WIDE),
            pltpu.VMEM((length, TILE), WIDE),
        ],
        cost_estimate=COST,
        name="attend_back",
    )(qkv, qkv, qkv, g, lse, seg_col, seg_row, cosine, sine)


def branch_kernel(count, at_ref, *refs):
    w_ref, out_ref, held, sems = refs[count:]

    @pl.when(pl.program_id(0) == 0)
    def _():
        load_shares(refs[:count], held, sems)

    out_ref[...] = dot(held[...], w_ref[...], NT)


def branch(shares, w_down, at):
    count, width, rows = len(shares), shares[0].shape[1], rows_in(shares)
    units = w_down.shape[0] // 2
    tiles = units // TILE
    return pl.pallas_call(
        functools.partial(branch_kernel, count),
        grid_spec=pltpu.PrefetchScalarGridSpec(
            num_scalar_prefetch=1,
            grid=(tiles,),
            in_specs=[pl.BlockSpec(memory_space=pl.ANY)] * count
            + [pl.BlockSpec((TILE, width), lambda i, at: (at[0] * tiles + i, 0))],
            out_specs=pl.BlockSpec((rows, TILE), lambda i, at: (0, i)),
            scratch_shapes=[
                pltpu.VMEM((rows, width), LOW),
                pltpu.SemaphoreType.DMA((count,)),
            ],
        ),
        out_shape=jax.ShapeDtypeStruct((rows, units), WIDE),
        cost_estimate=COST,
        name="branch",
    )(at, *shares, w_down)


def mix_kernel(count, at_ref, *refs):
    share_refs, (wg_ref, wu_ref, dm_ref) = refs[:count], refs[count : count + 3]
    m_ref, dg_ref, du_ref, held, sems = refs[-5:]

    @pl.when(pl.program_id(0) == 0)
    def _():
        load_shares(share_refs, held, sems)

    n = held[...]
    g = dot(n, wg_ref[...])
    u = dot(n, wu_ref[...])
    dm = dm_ref[...]
    s = jax.nn.sigmoid(g)
    active = g * s
    m_ref[...] = (active * u).astype(LOW)
    dg_ref[...] = (dm * u * s * (1.0 + g * (1.0 - s))).astype(LOW)
    du_ref[...] = (dm * active).astype(LOW)


def mix(shares, wg, wu, dm, at, block, given=()):
    count, width, rows = len(shares), shares[0].shape[1], rows_in(shares)
    tiles = dm.shape[1] // TILE
    weight = pl.BlockSpec((width, TILE), lambda i, at: (0, at[0] * tiles + i))
    spec = pl.BlockSpec((rows, TILE), lambda i, at: (block, i))
    return pl.pallas_call(
        functools.partial(mix_kernel, count),
        grid_spec=pltpu.PrefetchScalarGridSpec(
            num_scalar_prefetch=1,
            grid=(tiles,),
            in_specs=[pl.BlockSpec(memory_space=pl.ANY)] * count
            + [weight, weight, spec]
            + [pl.BlockSpec(memory_space=pl.ANY)] * len(given),
            out_specs=[spec] * 3,
            scratch_shapes=[
                pltpu.VMEM((rows, width), LOW),
                pltpu.SemaphoreType.DMA((count,)),
            ],
        ),
        out_shape=[jax.ShapeDtypeStruct(dm.shape, LOW)] * 3,
        input_output_aliases={count + 4 + i: i for i in range(len(given))},
        cost_estimate=COST,
        name="mix",
    )(at, *shares, wg, wu, dm, *given)


def unmix(dg, du, wg, wu, at, share):
    (rows, units), width = dg.shape, wg.shape[0]
    given = pl.BlockSpec((rows, units), lambda i, *_: (0, 0))
    moving = pl.BlockSpec((WIDE_TILE, units), lambda i, *_: (i, lax.axis_index("dp") // PAIR % 2))

    def compute(refs):
        _, dg_ref, du_ref, wg_ref, wu_ref = refs
        return dot(dg_ref[...], wg_ref[...], NT) + dot(du_ref[...], wu_ref[...], NT)

    specs = [given, given, moving, moving]
    return paired(compute, "unmix", rows // share, share, width, WIDE_TILE, specs, at, dg, du, wg, wu)


def down(m, w_down, at, share):
    rows, units = m.shape
    given = pl.BlockSpec((rows, units), lambda i, *_: (0, 0))
    moving = pl.BlockSpec((units, WIDE_TILE), lambda i, *_: (lax.axis_index("dp") // PAIR % 2, i))

    def compute(refs):
        _, m_ref, w_ref = refs
        return dot(m_ref[...], w_ref[...])

    width = w_down.shape[1]
    return paired(compute, "down", rows // share, share, width, WIDE_TILE, [given, moving], at, m, w_down)


class Shares:
    def __init__(self, shares, masks, place, order=None):
        self.shares, self.rows = list(shares), rows_in(shares)
        self.masks, self.place = masks, place
        self.blocks = jnp.array(block_order(masks), jnp.int32) ^ place
        sizes = [a.shape[0] for a in self.shares]
        if order is None:
            self.starts = jnp.array([sum(sizes[:i]) for i in range(len(sizes))], jnp.int32)
        else:
            self.starts = order * sizes[0]
        self.shape = (self.rows, self.shares[0].shape[1])

    def array(self):
        whole = jnp.zeros(self.shape, LOW)
        for i, a in enumerate(self.shares):
            piece = permute_columns(a, self.masks, self.place)
            whole = lax.dynamic_update_slice_in_dim(whole, piece, self.starts[i], 0)
        return whole


def block_copies(refs, starts_ref, blocks_ref, held, sems, low, width, j):
    source = pl.ds(pl.multiple_of(blocks_ref[low + j] * width, width), width)
    target = pl.ds(pl.multiple_of(j * width, width), width)
    for i, ref in enumerate(refs):
        first = pl.ds(pl.multiple_of(starts_ref[i], ref.shape[0]), ref.shape[0])
        yield pltpu.make_async_copy(ref.at[:, source], held.at[first, target], sems.at[j, i])


def product_rows(shares, starts, blocks, right, given, low, size, width, kind):
    count = len(shares)
    tokens, across = right.shape

    def kernel(starts_ref, blocks_ref, *refs):
        share_refs, right_ref, given_refs = refs[:count], refs[count], refs[count + 1 : -3]
        out_ref, held, sems = refs[-3:]
        i = pl.program_id(0)
        copies = functools.partial(block_copies, share_refs, starts_ref, blocks_ref, held, sems, low, width)

        @pl.when(i == 0)
        def _():
            for j in range(size):
                for copy in copies(j):
                    copy.start()

        for copy in copies(i):
            copy.wait()
        value = dot(held[:, pl.ds(pl.multiple_of(i * width, width), width)], right_ref[...], TN)
        for ref in given_refs:
            value = value + ref[...].astype(WIDE)
        out_ref[...] = value.astype(kind)

    return pl.pallas_call(
        kernel,
        grid_spec=pltpu.PrefetchScalarGridSpec(
            num_scalar_prefetch=2,
            grid=(size,),
            in_specs=[pl.BlockSpec(memory_space=pl.ANY)] * count
            + [pl.BlockSpec((tokens, across), lambda i, *_: (0, 0))]
            + [
                pl.BlockSpec((width, across), lambda i, *_, start=low - first: (start + i, 0))
                for first, _ in given
            ],
            out_specs=pl.BlockSpec((width, across), lambda i, *_: (i, 0)),
            scratch_shapes=[
                pltpu.VMEM((tokens, size * width), LOW),
                pltpu.SemaphoreType.DMA((size, count)),
            ],
        ),
        out_shape=jax.ShapeDtypeStruct((size * width, across), kind),
        cost_estimate=COST,
        name="product_rows",
    )(starts, blocks, *shares, right, *(array for _, array in given))


def product_cols(shares, starts, blocks, left, given, low, size, width, kind):
    count = len(shares)
    tokens, down_to = left.shape
    across = size * width
    tile = min(TILE, down_to)

    def kernel(starts_ref, blocks_ref, *refs):
        share_refs, left_ref, given_refs = refs[:count], refs[count], refs[count + 1 : -3]
        out_ref, held, sems = refs[-3:]
        copies = functools.partial(block_copies, share_refs, starts_ref, blocks_ref, held, sems, low, width)

        @pl.when(pl.program_id(0) == 0)
        def _():
            for j in range(size):
                for copy in copies(j):
                    copy.start()
            for j in range(size):
                for copy in copies(j):
                    copy.wait()

        value = dot(left_ref[...], held[...], TN)
        for ref in given_refs:
            value = value + ref[...].astype(WIDE)
        out_ref[...] = value.astype(kind)

    return pl.pallas_call(
        kernel,
        grid_spec=pltpu.PrefetchScalarGridSpec(
            num_scalar_prefetch=2,
            grid=(down_to // tile,),
            in_specs=[pl.BlockSpec(memory_space=pl.ANY)] * count
            + [pl.BlockSpec((tokens, tile), lambda i, *_: (0, i))]
            + [
                pl.BlockSpec((tile, across), lambda i, *_, start=(low - first) // size: (i, start))
                for first, _ in given
            ],
            out_specs=pl.BlockSpec((tile, across), lambda i, *_: (i, 0)),
            scratch_shapes=[
                pltpu.VMEM((tokens, across), LOW),
                pltpu.SemaphoreType.DMA((size, count)),
            ],
        ),
        out_shape=jax.ShapeDtypeStruct((down_to, across), kind),
        cost_estimate=COST,
        name="product_cols",
    )(starts, blocks, *shares, left, *(array for _, array in given))


def half_kernel(axis, at_ref, own_ref, other_ref, out_ref):
    size = own_ref.shape[axis]
    for ref, half in ((own_ref, at_ref[0]), (other_ref, 1 - at_ref[0])):
        where = pl.ds(pl.multiple_of(half * size, size), size)
        if axis == 0:
            out_ref[where, :] = ref[...].astype(WIDE)
        else:
            out_ref[:, where] = ref[...].astype(WIDE)


def halves(own, other, at, axis):
    shape = list(own.shape)
    shape[axis] *= 2
    return pl.pallas_call(
        functools.partial(half_kernel, axis),
        grid_spec=pltpu.PrefetchScalarGridSpec(
            num_scalar_prefetch=1,
            grid=(1,),
            in_specs=[pl.BlockSpec(own.shape, lambda i, at: (0, 0))] * 2,
            out_specs=pl.BlockSpec(tuple(shape), lambda i, at: (0, 0)),
        ),
        out_shape=jax.ShapeDtypeStruct(tuple(shape), WIDE),
        cost_estimate=COST,
        name="halves",
    )(at, own, other)


def whole(function, shapes, *arrays):
    def kernel(*refs):
        results = function(*(ref[...] for ref in refs[: len(arrays)]))
        for ref, value in zip(refs[len(arrays) :], results):
            ref[...] = value.astype(ref.dtype)

    return pl.pallas_call(
        kernel,
        out_shape=[jax.ShapeDtypeStruct(shape, kind) for shape, kind in shapes],
        in_specs=[pl.BlockSpec(memory_space=pltpu.VMEM)] * len(arrays),
        out_specs=[pl.BlockSpec(memory_space=pltpu.VMEM)] * len(shapes),
        cost_estimate=COST,
        name="whole",
    )(*arrays)


def norm_back_kernel(count, d_ref, value_ref, inverse_ref, gain_ref, *refs):
    term_refs, (dx_ref, low_ref, gain_out_ref) = refs[:count], refs[count:]
    d_normed = term_refs[0][...].astype(WIDE)
    for ref in term_refs[1:]:
        d_normed = d_normed + ref[...].astype(WIDE)
    values, inverse = value_ref[...].astype(WIDE), inverse_ref[...]
    scaled = d_normed * gain_ref[...].astype(WIDE)
    mean = jnp.mean(scaled * values, axis=-1, keepdims=True)
    dx = d_ref[...].astype(WIDE) + inverse * scaled - values * (inverse * inverse * inverse * mean)
    dx_ref[...] = dx.astype(dx_ref.dtype)
    low_ref[...] = (RESIDUAL_SCALE * dx).astype(LOW)

    @pl.when(pl.program_id(0) == 0)
    def _():
        gain_out_ref[...] = jnp.zeros_like(gain_out_ref)

    gain_out_ref[...] += jnp.sum(d_normed * values * inverse, axis=0, keepdims=True)


def norm_back(d_rows, values, inverse, gain, terms, kind, tile=64):
    rows, width = values.shape
    spec = pl.BlockSpec((tile, width), lambda i: (i, 0))
    fixed = pl.BlockSpec((1, width), lambda i: (0, 0))
    return pl.pallas_call(
        functools.partial(norm_back_kernel, len(terms)),
        grid=(rows // tile,),
        in_specs=[spec, spec, pl.BlockSpec((tile, 1), lambda i: (i, 0)), fixed] + [spec] * len(terms),
        out_specs=[spec, spec, fixed],
        out_shape=[
            jax.ShapeDtypeStruct((rows, width), kind),
            jax.ShapeDtypeStruct((rows, width), LOW),
            jax.ShapeDtypeStruct((1, width), WIDE),
        ],
        cost_estimate=COST,
        name="norm_back",
    )(d_rows, values, inverse, gain.reshape(1, -1), *terms)


def sum_all_kernel(steps, part_ref, out_ref, sent, got, send_sems, got_sems):
    partners = []
    for axis, mask in steps:
        mine = lax.axis_index(axis)
        partners.append({axis: mine + mask * (1 - 2 * (mine // mask % 2))})
    barrier = pltpu.get_barrier_semaphore()
    for partner in partners:
        pl.semaphore_signal(barrier, inc=1, device_id=partner, device_id_type=pl.DeviceIdType.MESH)
    pl.semaphore_wait(barrier, len(partners))
    total = part_ref[...]
    for i, partner in enumerate(partners):
        sent[i] = total
        copy = pltpu.make_async_remote_copy(
            src_ref=sent.at[i],
            dst_ref=got.at[i],
            send_sem=send_sems.at[i],
            recv_sem=got_sems.at[i],
            device_id=partner,
            device_id_type=pl.DeviceIdType.MESH,
        )
        copy.start()
        copy.wait()
        total = total + got[i]
    out_ref[...] = total


def sum_all(part, steps):
    count = len(steps)
    return pl.pallas_call(
        functools.partial(sum_all_kernel, steps),
        out_shape=jax.ShapeDtypeStruct(part.shape, part.dtype),
        in_specs=[pl.BlockSpec(memory_space=pltpu.VMEM)],
        out_specs=pl.BlockSpec(memory_space=pltpu.VMEM),
        scratch_shapes=[
            pltpu.VMEM((count, *part.shape), part.dtype),
            pltpu.VMEM((count, *part.shape), part.dtype),
            pltpu.SemaphoreType.DMA((count,)),
            pltpu.SemaphoreType.DMA((count,)),
        ],
        compiler_params=pltpu.CompilerParams(collective_id=IDS["sum_all"], has_side_effects=True),
        cost_estimate=COST,
        name="sum_all",
    )(part)


def swap(array, axis, mask):
    size = lax.axis_size(axis)
    return lax.ppermute(array, axis, [(i, i ^ mask) for i in range(size)])


def powers(size):
    return [1 << i for i in range(size.bit_length() - 1)]


def swap_both(array):
    count = lax.axis_size("tensor")
    size = lax.axis_size("dp") * count
    mask = PAIR * count + FAR
    return lax.ppermute(array, ("dp", "tensor"), [(i, i ^ mask) for i in range(size)])


def cut(array):
    half = array.shape[0] // 2
    return array[:half], array[half:]


def added(*arrays):
    total = arrays[0].astype(WIDE)
    for a in arrays[1:]:
        total = total + a.astype(WIDE)
    return total


def add_low(*arrays):
    return whole(lambda *a: (added(*a),), [(arrays[0].shape, LOW)], *arrays)[0]


def joined(mine, got):
    rows, width = mine.shape
    return whole(lambda a, b: cut(added(a, b)), [((rows // 2, width), LOW)] * 2, mine, got)


class GroupSum:
    def start_both(self, lane, both):
        low, high = lane(joined, *both)
        self.low, self.high = swap(low, "tensor", FAR), swap(high, "dp", PAIR)

    def start_far_pair(self, lane, own, far, pair):
        def relay(own, got_own, far, got_far, high, pair, got_pair, low):
            far, pair = added(far, got_far), added(pair, got_pair)
            rows = low.shape[0]
            far = jnp.concatenate([far[:rows], far[rows:] + high.astype(WIDE)], axis=0)
            pair = jnp.concatenate([pair[:rows] + low.astype(WIDE), pair[rows:]], axis=0)
            return added(own, got_own), far, pair

        self.own, far, pair = lane(
            functools.partial(whole, relay, [(own[0].shape, kind) for kind in (WIDE, LOW, LOW)]),
            *own,
            *far,
            self.high,
            *pair,
            self.low,
        )
        self.far, self.pair = swap(far, "tensor", FAR), swap(pair, "dp", PAIR)

    def terms(self):
        return self.own, self.far, self.pair


def block_order(masks):
    order = [0]
    for mask in reversed(masks):
        order = [mask ^ b for b in order] + order
    return order


def permute_columns(array, masks, place):
    count = 1 << len(masks)
    width = array.shape[1] // count
    return jnp.concatenate(
        [
            lax.dynamic_slice_in_dim(array, (place ^ b) * width, width, 1)
            for b in block_order(masks)
        ],
        axis=1,
    )


class Reduction:
    def __init__(self, shares, other, masks, axis):
        self.shares, self.other_side, self.masks, self.axis = shares, other, list(masks), axis
        self.count = 1 << len(masks)
        self.width = shares.shape[1] // self.count
        self.low, self.size, self.got = 0, self.count // 2, []

    def total(self, lane, low, high):
        firsts = [first for first, _ in self.got]
        width, axis = self.width, self.axis
        kind = WIDE if high == self.count else LOW
        arrays = [array for _, array in self.got]
        if width % LANES == 0:

            def compute(shares, starts, blocks, other, *arrays):
                product = product_cols if axis else product_rows
                given = list(zip(firsts, arrays))
                return product(shares, starts, blocks, other, given, low, high - low, width, kind)

            source = self.shares
            return lane(compute, source.shares, source.starts, source.blocks, self.other_side, *arrays)

        def compute(whole, other, *arrays):
            part = whole[:, low * width : high * width]
            value = dot(other, part, TN) if axis else dot(part, other, TN)
            for first, array in zip(firsts, arrays):
                piece = lax.slice_in_dim(
                    array, (low - first) * width, (high - first) * width, axis=axis
                )
                value = value + piece.astype(WIDE)
            return value.astype(kind)

        return lane(compute, self.shares.array(), self.other_side, *arrays)

    def step(self, lane):
        sent = self.total(lane, self.low, self.low + self.size)
        self.low += self.size
        self.size //= 2
        self.got.append((self.low, swap(sent, "dp", self.masks.pop(0))))
        return self

    def finish(self, lane):
        while self.masks:
            self.step(lane)
        return self.total(lane, self.low, self.count)

    def step_half(self, lane):
        while len(self.masks) > 1:
            self.step(lane)
        sent = self.total(lane, self.low, self.low + self.size)
        self.low += self.size
        self.partner = swap(sent, "dp", self.masks.pop(0))
        return self

    def finish_half(self, lane, at):
        own = self.total(lane, self.low, self.count)
        return lane(lambda a, b, at: halves(a, b, at, 1 - self.axis), own, self.partner, at)


def rows_of(shares):
    return jnp.concatenate(shares, axis=0)


def inverse_rms(value_rows):
    return lax.rsqrt(jnp.mean(value_rows * value_rows, axis=-1, keepdims=True) + EPSILON)


def body(
    layer_in,
    cotangent,
    segments,
    gain_attn,
    w_query,
    key_weight,
    value_weight,
    w_out,
    gain_ffn,
    w_gate,
    w_up,
    w_down,
):
    share, width = layer_in.shape
    count = lax.axis_size("tensor")
    rank = lax.axis_index("tensor")
    place = lax.axis_index("dp")
    masks = powers(lax.axis_size("dp"))
    group_masks = [m for m in masks if m != PAIR] + [PAIR]
    at = place // PAIR % 2
    at_array = at.reshape(1).astype(jnp.int32)
    order = jnp.arange(count, dtype=jnp.int32) ^ rank
    seqs = segments.shape[0]
    q_width, kv_width = w_query.shape[1], key_weight.shape[1]
    rows = count * share
    lane = Lane()


    def first_norm(layer_in, gain):
        x = layer_in.astype(WIDE)
        inverse = inverse_rms(x)
        return (x * inverse * gain.astype(WIDE)).astype(LOW), inverse

    n1_own, inverse_one = lane(first_norm, layer_in, gain_attn)
    n1_far = swap(n1_own, "tensor", FAR)

    def prepare(segments, w_query, key_weight, value_weight, cotangent):
        tables = rope_tables(positions_of(segments).reshape(-1))
        w_qkv = jnp.concatenate([w_query, key_weight, value_weight], axis=1)
        seg_col, seg_row = segments.reshape(-1, 1), segments[:, None, :]
        branch_own = (RESIDUAL_SCALE * cotangent.astype(WIDE)).astype(LOW)
        return tables, w_qkv, seg_col, seg_row, branch_own

    tables, w_qkv, seg_col, seg_row, branch_own = lane(
        prepare, segments, w_query, key_weight, value_weight, cotangent
    )
    turned = q_width + kv_width
    qkv, n1_near = lane(
        lambda a, order, w, c, s: project(a, order, w, rows, NN, "near_in", turned, (c, s)),
        n1_own,
        order[:2],
        w_qkv,
        *tables,
    )
    n1_far = after(n1_far, qkv)
    branch_own = after(branch_own, n1_far)
    branch_chips = [
        branch_own,
        swap_both(branch_own),
        swap(branch_own, "tensor", FAR),
        swap(branch_own, "dp", PAIR),
    ]
    qkv, n1_other = lane(
        lambda a, order, w, c, s, q: project(a, order, w, rows, NN, "far_in", turned, (c, s), (q,)),
        n1_far,
        order[2:],
        w_qkv,
        *tables,
        qkv,
    )
    attended, lse = lane(
        lambda q, c, r: attend(q, q_width, kv_width, c, r, seqs), qkv, seg_col, seg_row
    )
    own_terms, far_terms = lane(
        lambda a, w, o: pieces(a, w, o, count, NN, "out_pieces"), attended, w_out, order
    )
    got_far = swap(lane(add_low, *far_terms), "tensor", FAR)

    branch_chips = after(tuple(branch_chips), *lane.last)
    branch_shares = [b for a in branch_chips for b in (a, swap(a, "tensor", NEAR))]
    d_mixed = lane(lambda a, w, at: branch(a, w, at), branch_shares, w_down, at_array)

    def second_norm(layer_in, mine, near, far, gain):
        hidden = layer_in.astype(WIDE) + RESIDUAL_SCALE * added(mine, near, far)
        inverse = inverse_rms(hidden)
        return hidden, inverse, (hidden * inverse * gain.astype(WIDE)).astype(LOW)

    hidden, inverse_two, n2_own = lane(
        second_norm, layer_in, *own_terms, got_far, gain_ffn
    )
    n2_far, n2_pair = swap(n2_own, "tensor", FAR), swap(n2_own, "dp", PAIR)
    n2_own = [n2_own, swap(n2_own, "tensor", NEAR)]
    blend = lambda block: lambda a, g, u, d, at, *m: mix(a, g, u, d, at, block, m)
    mixed = lane(blend(0), n2_own, w_gate, w_up, d_mixed, at_array)
    n2_far, n2_pair = after((n2_far, n2_pair), mixed)
    n2_both = [swap(cut(n2_pair)[0], "tensor", FAR), swap(cut(n2_far)[1], "dp", PAIR)]
    n2_four = [n2_far, swap(n2_far, "tensor", NEAR), n2_pair, swap(n2_pair, "tensor", NEAR)]
    mixed = lane(blend(1), n2_four, w_gate, w_up, d_mixed, at_array, *mixed)
    n2_both = list(after(tuple(n2_both), *lane.last))
    n2_both = n2_both + [swap(a, "tensor", NEAR) for a in n2_both]
    mixed, d_gate, d_upper = lane(blend(1), n2_both, w_gate, w_up, d_mixed, at_array, *mixed)

    n2 = Shares(n2_own + n2_both + n2_four, group_masks, place)
    grad_down = Reduction(Shares(branch_shares, group_masks, place), mixed, group_masks, 1).step(lane)
    dn_parts = lane(
        lambda dg, du, wg, wu, at: unmix(dg, du, wg, wu, at, share),
        d_gate,
        d_upper,
        w_gate,
        w_up,
        at_array,
    )
    d_normed = GroupSum()
    d_normed.start_both(lane, dn_parts[1])
    grad_gate = Reduction(n2, d_gate, group_masks, 0).step(lane)
    d_normed.start_far_pair(lane, dn_parts[0], dn_parts[2], dn_parts[3])
    grad_up = Reduction(n2, d_upper, group_masks, 0).step(lane)
    grad_down.step(lane)
    ffn_parts = lane(lambda m, w, at: down(m, w, at, share), mixed, w_down, at_array)
    d_hidden, da_own, gain_two_part = lane(
        lambda c, h, i, g, *t: norm_back(c, h, i, g, t, WIDE),
        cotangent,
        hidden,
        inverse_two,
        gain_ffn,
        *d_normed.terms(),
    )
    da_far = swap(da_own, "tensor", FAR)
    n1_shares = [n1_own, n1_near, n1_far, n1_other]
    n1 = Shares(n1_shares, masks, place, order)
    d_attn, da_near = lane(
        lambda a, o, w: project(a, o, w, rows, NT, "near_back"), da_own, order[:2], w_out
    )
    grad_gate.step(lane)
    d_attn, da_other = lane(
        lambda a, o, w, d: project(a, o, w, rows, NT, "far_back", given=(d,)),
        da_far,
        order[2:],
        w_out,
        d_attn,
    )
    out_total = GroupSum()
    out_total.start_both(lane, ffn_parts[1])
    grad_down.step_half(lane)
    d_qkv = lane(
        lambda q, g, l, c, r, a, b: attend_back(q, q_width, kv_width, g, l, c, r, a, b, seqs),
        qkv,
        d_attn,
        lse,
        seg_col,
        seg_row,
        *tables,
    )
    grad_qkv = Reduction(n1, d_qkv, masks, 0).step(lane)
    grad_up.step(lane)
    out_total.start_far_pair(lane, ffn_parts[0], ffn_parts[2], ffn_parts[3])
    own_terms, far_terms = lane(
        lambda a, w, o: pieces(a, w, o, count, NT, "in_pieces"), d_qkv, w_qkv, order
    )
    got_far = swap(lane(add_low, *far_terms), "tensor", FAR)
    grad_gate.step_half(lane)
    grad_down = grad_down.finish_half(lane, at_array)
    grad_rows, _, gain_one_part = lane(
        lambda c, h, i, g, *t: norm_back(c, h, i, g, t, LOW),
        d_hidden,
        layer_in,
        inverse_one,
        gain_attn,
        *own_terms,
        got_far,
    )
    grad_gate = grad_gate.finish_half(lane, at_array)
    grad_qkv.step(lane)
    da = Shares([da_own, da_near, da_far, da_other], masks, place, order)
    grad_wout = Reduction(da, attended, masks, 1).step(lane)
    grad_up.step_half(lane)
    out_rows = lane(
        lambda hidden, *terms: whole(
            lambda hidden, *terms: (hidden + RESIDUAL_SCALE * added(*terms),),
            [(hidden.shape, LOW)],
            hidden,
            *terms,
        )[0],
        hidden,
        *out_total.terms(),
    )
    grad_wout.step(lane)
    grad_qkv.step(lane)
    grad_up = grad_up.finish_half(lane, at_array)
    grad_wout.step(lane)
    grad_qkv = grad_qkv.finish(lane)
    steps = [("tensor", m) for m in powers(count)] + [("dp", m) for m in masks]
    gains = lane(
        lambda a, b: sum_all(jnp.concatenate([a, b], axis=0), steps), gain_one_part, gain_two_part
    )
    block = width // lax.axis_size("dp")
    gains = lax.dynamic_slice_in_dim(gains, place * block, block, 1)
    grad_wout = grad_wout.finish(lane)
    return (
        out_rows,
        grad_rows,
        gains[0],
        grad_qkv[:, :q_width],
        grad_qkv[:, q_width : q_width + kv_width],
        grad_qkv[:, q_width + kv_width :],
        grad_wout,
        gains[1],
        grad_gate,
        grad_up,
        grad_down,
    )


def solution(mesh):
    return jax.shard_map(
        body,
        mesh=mesh,
        in_specs=(
            P(("dp", "tensor"), None),
            P(("dp", "tensor"), None),
            P("dp", None),
            P(),
            P(None, "tensor"),
            P(None, "tensor"),
            P(None, "tensor"),
            P("tensor", None),
            P(),
            P(None, "tensor"),
            P(None, "tensor"),
            P("tensor", None),
        ),
        out_specs=(
            P(("dp", "tensor"), None),
            P(("dp", "tensor"), None),
            P("dp"),
            P("dp", "tensor"),
            P("dp", "tensor"),
            P("dp", "tensor"),
            P("tensor", "dp"),
            P("dp"),
            P("dp", "tensor"),
            P("dp", "tensor"),
            P("tensor", "dp"),
        ),
        check_vma=False,
    )
```

```python
import functools

import jax
import jax.numpy as jnp
from jax import lax
from jax.experimental import pallas as pl
from jax.experimental.pallas import tpu as pltpu
from jax.sharding import PartitionSpec as P

HEAD_SIZE = 64


EPSILON = 1e-05
MULTIPLIER = 0.015625
RESIDUAL_SCALE = 0.22
THETA_BASE = 10000.0
MASK_VALUE = -1e30
LOW = jnp.bfloat16
WIDE = jnp.float32
LANES = 128
TILE = 256
WIDE_TILE = 512

NEAR, FAR, PAIR = 1, 2, 2
NN = (((1,), (0,)), ((), ()))
NT = (((1,), (1,)), ((), ()))
TN = (((0,), (0,)), ((), ()))
COST = pl.CostEstimate(flops=1, bytes_accessed=1, transcendentals=0)
IDS = {
    "sum_all": 0,
    "near_in": 1,
    "far_in": 2,
    "near_back": 3,
    "far_back": 4,
    "out_pieces": 5,
    "in_pieces": 6,
    "unmix": 7,
    "down": 8,
}


def dot(a, b, dims=NN):
    return lax.dot_general(a, b, dims, preferred_element_type=WIDE)


def after(value, *others):
    return lax.optimization_barrier((value, *others))[0]


class Lane:
    def __init__(self):
        self.last = ()

    def __call__(self, function, *operands):
        if self.last:
            operands = after(operands, *self.last)
        result = function(*operands)
        self.last = tuple(jax.tree.leaves(result))
        return result


def positions_of(seg_ids):
    length = seg_ids.shape[-1]
    index = jnp.broadcast_to(jnp.arange(length, dtype=jnp.int32), seg_ids.shape)
    before = jnp.concatenate([seg_ids[:, :1] - 1, seg_ids[:, :-1]], axis=1)
    starts = jnp.where(seg_ids != before, index, jnp.zeros_like(index))
    return index - lax.cummax(starts, axis=1)


def rope_tables(positions):
    half = HEAD_SIZE // 2
    freq = THETA_BASE ** (-2.0 * jnp.arange(half, dtype=jnp.float32) / HEAD_SIZE)
    angle = positions.astype(jnp.float32)[:, None] * freq[None, :]
    cosine, sine = jnp.cos(angle), jnp.sin(angle)
    repeats = LANES // HEAD_SIZE
    return (
        jnp.concatenate([cosine, cosine] * repeats, axis=1),
        jnp.concatenate([-sine, sine] * repeats, axis=1),
    )


def lane_index(shape):
    return lax.broadcasted_iota(jnp.int32, shape, len(shape) - 1)


def turn(u, cosine, sine):
    quarter = HEAD_SIZE // 2
    first = lane_index(u.shape) % HEAD_SIZE < quarter
    other = jnp.where(
        first, pltpu.roll(u, u.shape[1] - quarter, 1), pltpu.roll(u, quarter, 1)
    )
    return u * cosine + other * sine


def load_shares(share_refs, held, sems):
    copies, first = [], 0
    for i, ref in enumerate(share_refs):
        copies.append(pltpu.make_async_copy(ref, held.at[pl.ds(first, ref.shape[0])], sems.at[i]))
        first += ref.shape[0]
    for copy in copies:
        copy.start()
    for copy in copies:
        copy.wait()


def rows_in(shares):
    return sum(a.shape[0] for a in shares)


def near_core():
    mine = lax.axis_index("tensor")
    return {"tensor": mine + NEAR * (1 - 2 * (mine // NEAR % 2))}


def meet(partner):
    barrier = pltpu.get_barrier_semaphore()
    pl.semaphore_signal(barrier, inc=1, device_id=partner, device_id_type=pl.DeviceIdType.MESH)
    pl.semaphore_wait(barrier, 1)


def project_kernel(turned, dims, order_ref, share_ref, w_ref, *refs):
    tables = refs[:2]
    out_ref, other_ref, held, sems = refs[-4:]
    i, partner = pl.program_id(0), near_core()
    load = pltpu.make_async_copy(share_ref, held.at[0], sems.at[0])
    send = pltpu.make_async_remote_copy(
        src_ref=share_ref,
        dst_ref=other_ref,
        send_sem=sems.at[1],
        recv_sem=sems.at[2],
        device_id=partner,
        device_id_type=pl.DeviceIdType.MESH,
    )
    load_other = pltpu.make_async_copy(other_ref, held.at[1], sems.at[3])

    @pl.when(i == 0)
    def _():
        load.start()
        meet(partner)
        send.start()
        load.wait()

    @pl.when(i == 1)
    def _():
        send.wait()
        load_other.start()
        load_other.wait()

    out = dot(held[i], w_ref[...], dims)
    for j in range(out.shape[1] // LANES):
        part = out[:, j * LANES : (j + 1) * LANES]
        if j * LANES < turned:
            part = turn(part, tables[0][...], tables[1][...])
        out_ref[:, j * LANES : (j + 1) * LANES] = part.astype(LOW)


def project(own, order, weight, rows, dims, name, turned=0, tables=(), given=()):
    share, width = own.shape
    columns = weight.shape[1] if dims is NN else weight.shape[0]

    def moving(i, *_):
        mine = lax.axis_index("tensor")
        if "far" in name:
            mine = mine + FAR * (1 - 2 * (mine // FAR % 2))
        return mine + NEAR * (1 - 2 * (mine // NEAR % 2)) * i, 0

    return pl.pallas_call(
        functools.partial(project_kernel, turned, dims),
        grid_spec=pltpu.PrefetchScalarGridSpec(
            num_scalar_prefetch=1,
            grid=(2,),
            in_specs=[pl.BlockSpec(memory_space=pl.ANY)]
            + [pl.BlockSpec(weight.shape, lambda i, order: (0, 0))]
            + [pl.BlockSpec((share, LANES), moving)] * len(tables)
            + [pl.BlockSpec(memory_space=pl.ANY)] * len(given),
            out_specs=[pl.BlockSpec((share, columns), moving), pl.BlockSpec(memory_space=pl.ANY)],
            scratch_shapes=[
                pltpu.VMEM((2, share, width), LOW),
                pltpu.SemaphoreType.DMA((4,)),
            ],
        ),
        out_shape=[
            jax.ShapeDtypeStruct((rows, columns), LOW),
            jax.ShapeDtypeStruct(own.shape, LOW),
        ],
        input_output_aliases={3 + len(tables): 0} if given else {},
        compiler_params=pltpu.CompilerParams(collective_id=IDS[name], has_side_effects=True),
        cost_estimate=COST,
        name=name,
    )(order, own, weight, *tables, *given)


def paired_kernel(compute, count, share, *refs):
    half = count // 2
    got_refs, sent, send_sems, got_sems = refs[-3 - half : -3], *refs[-3:]
    mine_refs = refs[-3 - 2 * half : -3 - half]
    i, steps, partner = pl.program_id(0), pl.num_programs(0), near_core()
    tile = mine_refs[0].shape[1]

    def copy(step, k):
        columns = pl.ds(pl.multiple_of(step * tile, tile), tile)
        return pltpu.make_async_remote_copy(
            src_ref=sent.at[step % 2, k],
            dst_ref=got_refs[k].at[:, columns],
            send_sem=send_sems.at[step % 2, k],
            recv_sem=got_sems.at[step, k],
            device_id=partner,
            device_id_type=pl.DeviceIdType.MESH,
        )

    @pl.when(i == 0)
    def _():
        meet(partner)

    total = compute(refs[: -3 - 2 * half])
    for k in range(half):
        mine_refs[k][...] = total[2 * k * share : (2 * k + 1) * share].astype(LOW)

    @pl.when(i >= 2)
    def _():
        for k in range(half):
            copy(i - 2, k).wait_send()

    for k in range(half):
        sent[i % 2, k] = total[(2 * k + 1) * share : (2 * k + 2) * share].astype(LOW)

    @pl.when(i >= 1)
    def _():
        for k in range(half):
            copy(i - 1, k).start()

    @pl.when(i == steps - 1)
    def _():
        for k in range(half):
            copy(i, k).start()
        for k in range(half):
            copy(i - 1, k).wait_send()
            copy(i, k).wait_send()

        def arrived(step, carry):
            for k in range(half):
                copy(step, k).wait_recv()
            return carry

        lax.fori_loop(0, steps, arrived, 0)


def paired(compute, name, count, share, width, tile, in_specs, prefetch, *operands):
    half, steps = count // 2, width // tile
    piece = jax.ShapeDtypeStruct((share, width), LOW)
    results = pl.pallas_call(
        functools.partial(paired_kernel, compute, count, share),
        grid_spec=pltpu.PrefetchScalarGridSpec(
            num_scalar_prefetch=1,
            grid=(steps,),
            in_specs=in_specs,
            out_specs=[pl.BlockSpec((share, tile), lambda i, *_: (0, i))] * half
            + [pl.BlockSpec(memory_space=pl.ANY)] * half,
            scratch_shapes=[
                pltpu.VMEM((2, half, share, tile), LOW),
                pltpu.SemaphoreType.DMA((2, half)),
                pltpu.SemaphoreType.DMA((steps, half)),
            ],
        ),
        out_shape=[piece] * (2 * half),
        compiler_params=pltpu.CompilerParams(collective_id=IDS[name], has_side_effects=True),
        cost_estimate=COST,
        name=name,
    )(prefetch, *operands)
    return list(zip(results[:half], results[half:]))


def pieces(a, weight, order, count, dims, name):
    rows, depth = a.shape
    share = rows // count
    width = weight.shape[1] if dims is NN else weight.shape[0]
    tile = WIDE_TILE
    moving = (
        pl.BlockSpec((depth, tile), lambda i, *_: (0, i))
        if dims is NN
        else pl.BlockSpec((tile, depth), lambda i, *_: (i, 0))
    )

    def compute(refs):
        _, a_ref, w_ref = refs
        parts = []
        for i in range(count):
            block = lax.axis_index("tensor")
            for mask in powers(count):
                if i & mask:
                    block = block + mask * (1 - 2 * (block // mask % 2))
            parts.append(a_ref[pl.ds(pl.multiple_of(block * share, share), share), :])
        return dot(jnp.concatenate(parts, axis=0), w_ref[...], dims)

    given = pl.BlockSpec((rows, depth), lambda i, *_: (0, 0))
    return paired(compute, name, count, share, width, tile, [given, moving], order, a, weight)


def doubled(pair, half):
    swapped = pltpu.roll(pair.astype(WIDE), HEAD_SIZE, 1).astype(pair.dtype)
    low = lane_index(pair.shape) < HEAD_SIZE
    return jnp.where(low == (half == 0), pair, swapped)


def attend_kernel(per_kv, q_ref, k_ref, v_ref, segc_ref, segr_ref, o_ref, lse_ref, s_buf):
    half = (pl.program_id(1) // per_kv) % 2
    length = k_ref.shape[0]
    k, v = doubled(k_ref[...], half), doubled(v_ref[...], half)
    low = lane_index((TILE, LANES)) < HEAD_SIZE
    k_at = lax.broadcasted_iota(jnp.int32, (TILE, TILE), 0)
    q_at = lax.broadcasted_iota(jnp.int32, (TILE, TILE), 1)
    for i in range(length // TILE):
        rows = slice(i * TILE, (i + 1) * TILE)
        q = q_ref[rows, :]
        outs = []
        for head in range(2):
            mine = jnp.where(low == (head == 0), q, jnp.zeros_like(q))
            top = jnp.full((1, TILE), MASK_VALUE, WIDE)
            for j in range(i + 1):
                keys = slice(j * TILE, (j + 1) * TILE)
                allowed = segc_ref[keys, :] == segr_ref[:, rows]
                if i == j:
                    allowed = allowed & (k_at <= q_at)
                raw = dot(k[keys], mine, NT)
                scores = jnp.where(allowed, MULTIPLIER * raw, MASK_VALUE)
                top = jnp.maximum(top, jnp.max(scores, axis=0, keepdims=True))
                s_buf[head, keys, :] = scores
            total = jnp.zeros((1, TILE), WIDE)
            for j in range(i + 1):
                keys = slice(j * TILE, (j + 1) * TILE)
                e = jnp.exp(s_buf[head, keys, :] - top)
                total = total + jnp.sum(e, axis=0, keepdims=True)
                s_buf[head, keys, :] = e
            scale = 1.0 / total
            out = jnp.zeros((TILE, LANES), WIDE)
            for j in range(i + 1):
                keys = slice(j * TILE, (j + 1) * TILE)
                out = out + dot((s_buf[head, keys, :] * scale).astype(LOW), v[keys], TN)
            outs.append(out)
            lse_ref[0, head : head + 1, rows] = top + jnp.log(total)
        o_ref[rows, :] = jnp.where(low, outs[0], outs[1]).astype(LOW)


def attend(qkv, q_width, kv_width, seg_col, seg_row, seqs):
    rows = qkv.shape[0]
    length = rows // seqs
    pairs, kv_pairs = q_width // LANES, kv_width // LANES
    per_kv = pairs // kv_pairs // 2
    return pl.pallas_call(
        functools.partial(attend_kernel, per_kv),
        grid=(seqs, pairs),
        in_specs=[
            pl.BlockSpec((length, LANES), lambda s, h: (s, h)),
            pl.BlockSpec((length, LANES), lambda s, h: (s, pairs + h // (2 * per_kv))),
            pl.BlockSpec((length, LANES), lambda s, h: (s, pairs + kv_pairs + h // (2 * per_kv))),
            pl.BlockSpec((length, 1), lambda s, h: (s, 0)),
            pl.BlockSpec((None, 1, length), lambda s, h: (s, 0, 0)),
        ],
        out_specs=[
            pl.BlockSpec((length, LANES), lambda s, h: (s, h)),
            pl.BlockSpec((1, 2, length), lambda s, h: (h, 0, s)),
        ],
        out_shape=[
            jax.ShapeDtypeStruct((rows, q_width), LOW),
            jax.ShapeDtypeStruct((pairs, 2, rows), WIDE),
        ],
        scratch_shapes=[pltpu.VMEM((2, length, TILE), WIDE)],
        cost_estimate=COST,
        name="attend",
    )(qkv, qkv, qkv, seg_col, seg_row)


def attend_back_kernel(
    per_kv,
    q_ref,
    k_ref,
    v_ref,
    g_ref,
    lse_ref,
    segc_ref,
    segr_ref,
    cos_ref,
    sin_ref,
    out_ref,
    dk_acc,
    dv_acc,
    p_buf,
    dp_buf,
):
    pair, pairs = pl.program_id(1), pl.num_programs(1)
    slot = (pair // per_kv) % 2
    length = k_ref.shape[0]
    k, v = doubled(k_ref[...], slot), doubled(v_ref[...], slot)
    low = lane_index((TILE, LANES)) < HEAD_SIZE
    k_at = lax.broadcasted_iota(jnp.int32, (TILE, TILE), 0)
    q_at = lax.broadcasted_iota(jnp.int32, (TILE, TILE), 1)

    @pl.when(pair % per_kv == 0)
    def _():
        dk_acc[slot] = jnp.zeros_like(dk_acc[slot])
        dv_acc[slot] = jnp.zeros_like(dv_acc[slot])

    for i in range(length // TILE):
        rows = slice(i * TILE, (i + 1) * TILE)
        q, g = q_ref[rows, :], g_ref[rows, :]
        dq = []
        for head in range(2):
            chosen = low == (head == 0)
            qh = jnp.where(chosen, q, jnp.zeros_like(q))
            gh = jnp.where(chosen, g, jnp.zeros_like(g))
            lse = lse_ref[0, head : head + 1, rows]
            inner = jnp.zeros((1, TILE), WIDE)
            for j in range(i + 1):
                keys = slice(j * TILE, (j + 1) * TILE)
                allowed = segc_ref[keys, :] == segr_ref[:, rows]
                if i == j:
                    allowed = allowed & (k_at <= q_at)
                raw = dot(k[keys], qh, NT)
                p = jnp.exp(jnp.where(allowed, MULTIPLIER * raw, MASK_VALUE) - lse)
                dp = dot(v[keys], gh, NT)
                inner = inner + jnp.sum(p * dp, axis=0, keepdims=True)
                p_buf[keys, :] = p
                dp_buf[keys, :] = dp
            total = jnp.zeros((TILE, LANES), WIDE)
            for j in range(i + 1):
                keys = slice(j * TILE, (j + 1) * TILE)
                p = p_buf[keys, :]
                ds = (p * (dp_buf[keys, :] - inner)).astype(LOW)
                dv_acc[slot, keys, :] += dot(p.astype(LOW), gh)
                dk_acc[slot, keys, :] += dot(ds, qh)
                total = total + dot(ds, k[keys], TN)
            dq.append(total)
        out_ref[rows, pl.ds(pl.multiple_of(pair * LANES, LANES), LANES)] = turn(
            MULTIPLIER * jnp.where(low, dq[0], dq[1]), cos_ref[rows, :], -sin_ref[rows, :]
        ).astype(LOW)

    @pl.when(pair % (2 * per_kv) == 2 * per_kv - 1)
    def _():
        low_all = lane_index((length, LANES)) < HEAD_SIZE

        def folded(acc):
            a, b = acc[0], acc[1]
            a = a + pltpu.roll(a, HEAD_SIZE, 1)
            b = b + pltpu.roll(b, HEAD_SIZE, 1)
            return jnp.where(low_all, a, b)

        kv_pair = pair // (2 * per_kv)
        key_at = pl.multiple_of((pairs + kv_pair) * LANES, LANES)
        value_at = pl.multiple_of((pairs + pairs // (2 * per_kv) + kv_pair) * LANES, LANES)
        out_ref[:, pl.ds(key_at, LANES)] = turn(
            MULTIPLIER * folded(dk_acc), cos_ref[...], -sin_ref[...]
        ).astype(LOW)
        out_ref[:, pl.ds(value_at, LANES)] = folded(dv_acc).astype(LOW)


def attend_back(qkv, q_width, kv_width, g, lse, seg_col, seg_row, cosine, sine, seqs):
    rows = qkv.shape[0]
    length = rows // seqs
    pairs, kv_pairs = q_width // LANES, kv_width // LANES
    per_kv = pairs // kv_pairs // 2
    by_pair = lambda s, h: (s, h)
    by_seq = lambda s, h: (s, 0)
    return pl.pallas_call(
        functools.partial(attend_back_kernel, per_kv),
        grid=(seqs, pairs),
        in_specs=[
            pl.BlockSpec((length, LANES), by_pair),
            pl.BlockSpec((length, LANES), lambda s, h: (s, pairs + h // (2 * per_kv))),
            pl.BlockSpec((length, LANES), lambda s, h: (s, pairs + kv_pairs + h // (2 * per_kv))),
            pl.BlockSpec((length, LANES), by_pair),
            pl.BlockSpec((1, 2, length), lambda s, h: (h, 0, s)),
            pl.BlockSpec((length, 1), by_seq),
            pl.BlockSpec((None, 1, length), lambda s, h: (s, 0, 0)),
            pl.BlockSpec((length, LANES), by_seq),
            pl.BlockSpec((length, LANES), by_seq),
        ],
        out_specs=pl.BlockSpec((length, qkv.shape[1]), by_seq),
        out_shape=jax.ShapeDtypeStruct(qkv.shape, LOW),
        scratch_shapes=[
            pltpu.VMEM((2, length, LANES), WIDE),
            pltpu.VMEM((2, length, LANES), WIDE),
            pltpu.VMEM((length, TILE), WIDE),
            pltpu.VMEM((length, TILE), WIDE),
        ],
        cost_estimate=COST,
        name="attend_back",
    )(qkv, qkv, qkv, g, lse, seg_col, seg_row, cosine, sine)


def branch_kernel(count, at_ref, *refs):
    w_ref, out_ref, held, sems = refs[count:]

    @pl.when(pl.program_id(0) == 0)
    def _():
        load_shares(refs[:count], held, sems)

    out_ref[...] = dot(held[...], w_ref[...], NT)


def branch(shares, w_down, at):
    count, width, rows = len(shares), shares[0].shape[1], rows_in(shares)
    units = w_down.shape[0] // 2
    tiles = units // TILE
    return pl.pallas_call(
        functools.partial(branch_kernel, count),
        grid_spec=pltpu.PrefetchScalarGridSpec(
            num_scalar_prefetch=1,
            grid=(tiles,),
            in_specs=[pl.BlockSpec(memory_space=pl.ANY)] * count
            + [pl.BlockSpec((TILE, width), lambda i, at: (at[0] * tiles + i, 0))],
            out_specs=pl.BlockSpec((rows, TILE), lambda i, at: (0, i)),
            scratch_shapes=[
                pltpu.VMEM((rows, width), LOW),
                pltpu.SemaphoreType.DMA((count,)),
            ],
        ),
        out_shape=jax.ShapeDtypeStruct((rows, units), WIDE),
        cost_estimate=COST,
        name="branch",
    )(at, *shares, w_down)


def mix_kernel(count, at_ref, *refs):
    share_refs, (wg_ref, wu_ref, dm_ref) = refs[:count], refs[count : count + 3]
    m_ref, dg_ref, du_ref, held, sems = refs[-5:]

    @pl.when(pl.program_id(0) == 0)
    def _():
        load_shares(share_refs, held, sems)

    n = held[...]
    g = dot(n, wg_ref[...])
    u = dot(n, wu_ref[...])
    dm = dm_ref[...]
    s = jax.nn.sigmoid(g)
    active = g * s
    m_ref[...] = (active * u).astype(LOW)
    dg_ref[...] = (dm * u * s * (1.0 + g * (1.0 - s))).astype(LOW)
    du_ref[...] = (dm * active).astype(LOW)


def mix(shares, wg, wu, dm, at, block, given=()):
    count, width, rows = len(shares), shares[0].shape[1], rows_in(shares)
    tiles = dm.shape[1] // TILE
    weight = pl.BlockSpec((width, TILE), lambda i, at: (0, at[0] * tiles + i))
    spec = pl.BlockSpec((rows, TILE), lambda i, at: (block, i))
    return pl.pallas_call(
        functools.partial(mix_kernel, count),
        grid_spec=pltpu.PrefetchScalarGridSpec(
            num_scalar_prefetch=1,
            grid=(tiles,),
            in_specs=[pl.BlockSpec(memory_space=pl.ANY)] * count
            + [weight, weight, spec]
            + [pl.BlockSpec(memory_space=pl.ANY)] * len(given),
            out_specs=[spec] * 3,
            scratch_shapes=[
                pltpu.VMEM((rows, width), LOW),
                pltpu.SemaphoreType.DMA((count,)),
            ],
        ),
        out_shape=[jax.ShapeDtypeStruct(dm.shape, LOW)] * 3,
        input_output_aliases={count + 4 + i: i for i in range(len(given))},
        cost_estimate=COST,
        name="mix",
    )(at, *shares, wg, wu, dm, *given)


def unmix(dg, du, wg, wu, at, share):
    (rows, units), width = dg.shape, wg.shape[0]
    given = pl.BlockSpec((rows, units), lambda i, *_: (0, 0))
    moving = pl.BlockSpec((WIDE_TILE, units), lambda i, *_: (i, lax.axis_index("dp") // PAIR % 2))

    def compute(refs):
        _, dg_ref, du_ref, wg_ref, wu_ref = refs
        return dot(dg_ref[...], wg_ref[...], NT) + dot(du_ref[...], wu_ref[...], NT)

    specs = [given, given, moving, moving]
    return paired(compute, "unmix", rows // share, share, width, WIDE_TILE, specs, at, dg, du, wg, wu)


def down(m, w_down, at, share):
    rows, units = m.shape
    given = pl.BlockSpec((rows, units), lambda i, *_: (0, 0))
    moving = pl.BlockSpec((units, WIDE_TILE), lambda i, *_: (lax.axis_index("dp") // PAIR % 2, i))

    def compute(refs):
        _, m_ref, w_ref = refs
        return dot(m_ref[...], w_ref[...])

    width = w_down.shape[1]
    return paired(compute, "down", rows // share, share, width, WIDE_TILE, [given, moving], at, m, w_down)


class Shares:
    def __init__(self, shares, masks, place, order=None):
        self.shares, self.rows = list(shares), rows_in(shares)
        self.masks, self.place = masks, place
        self.blocks = jnp.array(block_order(masks), jnp.int32) ^ place
        sizes = [a.shape[0] for a in self.shares]
        if order is None:
            self.starts = jnp.array([sum(sizes[:i]) for i in range(len(sizes))], jnp.int32)
        else:
            self.starts = order * sizes[0]
        self.shape = (self.rows, self.shares[0].shape[1])

    def array(self):
        whole = jnp.zeros(self.shape, LOW)
        for i, a in enumerate(self.shares):
            piece = permute_columns(a, self.masks, self.place)
            whole = lax.dynamic_update_slice_in_dim(whole, piece, self.starts[i], 0)
        return whole


def block_copies(refs, starts_ref, blocks_ref, held, sems, low, width, j):
    source = pl.ds(pl.multiple_of(blocks_ref[low + j] * width, width), width)
    target = pl.ds(pl.multiple_of(j * width, width), width)
    for i, ref in enumerate(refs):
        first = pl.ds(pl.multiple_of(starts_ref[i], ref.shape[0]), ref.shape[0])
        yield pltpu.make_async_copy(ref.at[:, source], held.at[first, target], sems.at[j, i])


def product_rows(shares, starts, blocks, right, given, low, size, width, kind):
    count = len(shares)
    tokens, across = right.shape

    def kernel(starts_ref, blocks_ref, *refs):
        share_refs, right_ref, given_refs = refs[:count], refs[count], refs[count + 1 : -3]
        out_ref, held, sems = refs[-3:]
        i = pl.program_id(0)
        copies = functools.partial(block_copies, share_refs, starts_ref, blocks_ref, held, sems, low, width)

        @pl.when(i == 0)
        def _():
            for j in range(size):
                for copy in copies(j):
                    copy.start()

        for copy in copies(i):
            copy.wait()
        value = dot(held[:, pl.ds(pl.multiple_of(i * width, width), width)], right_ref[...], TN)
        for ref in given_refs:
            value = value + ref[...].astype(WIDE)
        out_ref[...] = value.astype(kind)

    return pl.pallas_call(
        kernel,
        grid_spec=pltpu.PrefetchScalarGridSpec(
            num_scalar_prefetch=2,
            grid=(size,),
            in_specs=[pl.BlockSpec(memory_space=pl.ANY)] * count
            + [pl.BlockSpec((tokens, across), lambda i, *_: (0, 0))]
            + [
                pl.BlockSpec((width, across), lambda i, *_, start=low - first: (start + i, 0))
                for first, _ in given
            ],
            out_specs=pl.BlockSpec((width, across), lambda i, *_: (i, 0)),
            scratch_shapes=[
                pltpu.VMEM((tokens, size * width), LOW),
                pltpu.SemaphoreType.DMA((size, count)),
            ],
        ),
        out_shape=jax.ShapeDtypeStruct((size * width, across), kind),
        cost_estimate=COST,
        name="product_rows",
    )(starts, blocks, *shares, right, *(array for _, array in given))


def product_cols(shares, starts, blocks, left, given, low, size, width, kind):
    count = len(shares)
    tokens, down_to = left.shape
    across = size * width
    tile = min(TILE, down_to)

    def kernel(starts_ref, blocks_ref, *refs):
        share_refs, left_ref, given_refs = refs[:count], refs[count], refs[count + 1 : -3]
        out_ref, held, sems = refs[-3:]
        copies = functools.partial(block_copies, share_refs, starts_ref, blocks_ref, held, sems, low, width)

        @pl.when(pl.program_id(0) == 0)
        def _():
            for j in range(size):
                for copy in copies(j):
                    copy.start()
            for j in range(size):
                for copy in copies(j):
                    copy.wait()

        value = dot(left_ref[...], held[...], TN)
        for ref in given_refs:
            value = value + ref[...].astype(WIDE)
        out_ref[...] = value.astype(kind)

    return pl.pallas_call(
        kernel,
        grid_spec=pltpu.PrefetchScalarGridSpec(
            num_scalar_prefetch=2,
            grid=(down_to // tile,),
            in_specs=[pl.BlockSpec(memory_space=pl.ANY)] * count
            + [pl.BlockSpec((tokens, tile), lambda i, *_: (0, i))]
            + [
                pl.BlockSpec((tile, across), lambda i, *_, start=(low - first) // size: (i, start))
                for first, _ in given
            ],
            out_specs=pl.BlockSpec((tile, across), lambda i, *_: (i, 0)),
            scratch_shapes=[
                pltpu.VMEM((tokens, across), LOW),
                pltpu.SemaphoreType.DMA((size, count)),
            ],
        ),
        out_shape=jax.ShapeDtypeStruct((down_to, across), kind),
        cost_estimate=COST,
        name="product_cols",
    )(starts, blocks, *shares, left, *(array for _, array in given))


def half_kernel(axis, at_ref, own_ref, other_ref, out_ref):
    size = own_ref.shape[axis]
    for ref, half in ((own_ref, at_ref[0]), (other_ref, 1 - at_ref[0])):
        where = pl.ds(pl.multiple_of(half * size, size), size)
        if axis == 0:
            out_ref[where, :] = ref[...].astype(WIDE)
        else:
            out_ref[:, where] = ref[...].astype(WIDE)


def halves(own, other, at, axis):
    shape = list(own.shape)
    shape[axis] *= 2
    return pl.pallas_call(
        functools.partial(half_kernel, axis),
        grid_spec=pltpu.PrefetchScalarGridSpec(
            num_scalar_prefetch=1,
            grid=(1,),
            in_specs=[pl.BlockSpec(own.shape, lambda i, at: (0, 0))] * 2,
            out_specs=pl.BlockSpec(tuple(shape), lambda i, at: (0, 0)),
        ),
        out_shape=jax.ShapeDtypeStruct(tuple(shape), WIDE),
        cost_estimate=COST,
        name="halves",
    )(at, own, other)


def whole(function, shapes, *arrays):
    def kernel(*refs):
        results = function(*(ref[...] for ref in refs[: len(arrays)]))
        for ref, value in zip(refs[len(arrays) :], results):
            ref[...] = value.astype(ref.dtype)

    return pl.pallas_call(
        kernel,
        out_shape=[jax.ShapeDtypeStruct(shape, kind) for shape, kind in shapes],
        in_specs=[pl.BlockSpec(memory_space=pltpu.VMEM)] * len(arrays),
        out_specs=[pl.BlockSpec(memory_space=pltpu.VMEM)] * len(shapes),
        cost_estimate=COST,
        name="whole",
    )(*arrays)


def norm_back_kernel(count, d_ref, value_ref, inverse_ref, gain_ref, *refs):
    term_refs, (dx_ref, low_ref, gain_out_ref) = refs[:count], refs[count:]
    d_normed = term_refs[0][...].astype(WIDE)
    for ref in term_refs[1:]:
        d_normed = d_normed + ref[...].astype(WIDE)
    values, inverse = value_ref[...].astype(WIDE), inverse_ref[...]
    scaled = d_normed * gain_ref[...].astype(WIDE)
    mean = jnp.mean(scaled * values, axis=-1, keepdims=True)
    dx = d_ref[...].astype(WIDE) + inverse * scaled - values * (inverse * inverse * inverse * mean)
    dx_ref[...] = dx.astype(dx_ref.dtype)
    low_ref[...] = (RESIDUAL_SCALE * dx).astype(LOW)

    @pl.when(pl.program_id(0) == 0)
    def _():
        gain_out_ref[...] = jnp.zeros_like(gain_out_ref)

    gain_out_ref[...] += jnp.sum(d_normed * values * inverse, axis=0, keepdims=True)


def norm_back(d_rows, values, inverse, gain, terms, kind, tile=64):
    rows, width = values.shape
    spec = pl.BlockSpec((tile, width), lambda i: (i, 0))
    fixed = pl.BlockSpec((1, width), lambda i: (0, 0))
    return pl.pallas_call(
        functools.partial(norm_back_kernel, len(terms)),
        grid=(rows // tile,),
        in_specs=[spec, spec, pl.BlockSpec((tile, 1), lambda i: (i, 0)), fixed] + [spec] * len(terms),
        out_specs=[spec, spec, fixed],
        out_shape=[
            jax.ShapeDtypeStruct((rows, width), kind),
            jax.ShapeDtypeStruct((rows, width), LOW),
            jax.ShapeDtypeStruct((1, width), WIDE),
        ],
        cost_estimate=COST,
        name="norm_back",
    )(d_rows, values, inverse, gain.reshape(1, -1), *terms)


def sum_all_kernel(steps, part_ref, out_ref, sent, got, send_sems, got_sems):
    partners = []
    for axis, mask in steps:
        mine = lax.axis_index(axis)
        partners.append({axis: mine + mask * (1 - 2 * (mine // mask % 2))})
    barrier = pltpu.get_barrier_semaphore()
    for partner in partners:
        pl.semaphore_signal(barrier, inc=1, device_id=partner, device_id_type=pl.DeviceIdType.MESH)
    pl.semaphore_wait(barrier, len(partners))
    total = part_ref[...]
    for i, partner in enumerate(partners):
        sent[i] = total
        copy = pltpu.make_async_remote_copy(
            src_ref=sent.at[i],
            dst_ref=got.at[i],
            send_sem=send_sems.at[i],
            recv_sem=got_sems.at[i],
            device_id=partner,
            device_id_type=pl.DeviceIdType.MESH,
        )
        copy.start()
        copy.wait()
        total = total + got[i]
    out_ref[...] = total


def sum_all(part, steps):
    count = len(steps)
    return pl.pallas_call(
        functools.partial(sum_all_kernel, steps),
        out_shape=jax.ShapeDtypeStruct(part.shape, part.dtype),
        in_specs=[pl.BlockSpec(memory_space=pltpu.VMEM)],
        out_specs=pl.BlockSpec(memory_space=pltpu.VMEM),
        scratch_shapes=[
            pltpu.VMEM((count, *part.shape), part.dtype),
            pltpu.VMEM((count, *part.shape), part.dtype),
            pltpu.SemaphoreType.DMA((count,)),
            pltpu.SemaphoreType.DMA((count,)),
        ],
        compiler_params=pltpu.CompilerParams(collective_id=IDS["sum_all"], has_side_effects=True),
        cost_estimate=COST,
        name="sum_all",
    )(part)


def swap(array, axis, mask):
    size = lax.axis_size(axis)
    return lax.ppermute(array, axis, [(i, i ^ mask) for i in range(size)])


def powers(size):
    return [1 << i for i in range(size.bit_length() - 1)]


def swap_both(array):
    count = lax.axis_size("tensor")
    size = lax.axis_size("dp") * count
    mask = PAIR * count + FAR
    return lax.ppermute(array, ("dp", "tensor"), [(i, i ^ mask) for i in range(size)])


def cut(array):
    half = array.shape[0] // 2
    return array[:half], array[half:]


def added(*arrays):
    total = arrays[0].astype(WIDE)
    for a in arrays[1:]:
        total = total + a.astype(WIDE)
    return total


def add_low(*arrays):
    return whole(lambda *a: (added(*a),), [(arrays[0].shape, LOW)], *arrays)[0]


def joined(mine, got):
    rows, width = mine.shape
    return whole(lambda a, b: cut(added(a, b)), [((rows // 2, width), LOW)] * 2, mine, got)


class GroupSum:
    def start_both(self, lane, both):
        low, high = lane(joined, *both)
        self.low, self.high = swap(low, "tensor", FAR), swap(high, "dp", PAIR)

    def start_far_pair(self, lane, own, far, pair):
        def relay(own, got_own, far, got_far, high, pair, got_pair, low):
            far, pair = added(far, got_far), added(pair, got_pair)
            rows = low.shape[0]
            far = jnp.concatenate([far[:rows], far[rows:] + high.astype(WIDE)], axis=0)
            pair = jnp.concatenate([pair[:rows] + low.astype(WIDE), pair[rows:]], axis=0)
            return added(own, got_own), far, pair

        self.own, far, pair = lane(
            functools.partial(whole, relay, [(own[0].shape, kind) for kind in (WIDE, LOW, LOW)]),
            *own,
            *far,
            self.high,
            *pair,
            self.low,
        )
        self.far, self.pair = swap(far, "tensor", FAR), swap(pair, "dp", PAIR)

    def terms(self):
        return self.own, self.far, self.pair


def block_order(masks):
    order = [0]
    for mask in reversed(masks):
        order = [mask ^ b for b in order] + order
    return order


def permute_columns(array, masks, place):
    count = 1 << len(masks)
    width = array.shape[1] // count
    return jnp.concatenate(
        [
            lax.dynamic_slice_in_dim(array, (place ^ b) * width, width, 1)
            for b in block_order(masks)
        ],
        axis=1,
    )


class Reduction:
    def __init__(self, shares, other, masks, axis):
        self.shares, self.other_side, self.masks, self.axis = shares, other, list(masks), axis
        self.count = 1 << len(masks)
        self.width = shares.shape[1] // self.count
        self.low, self.size, self.got = 0, self.count // 2, []

    def total(self, lane, low, high):
        firsts = [first for first, _ in self.got]
        width, axis = self.width, self.axis
        kind = WIDE if high == self.count else LOW
        arrays = [array for _, array in self.got]
        if width % LANES == 0:

            def compute(shares, starts, blocks, other, *arrays):
                product = product_cols if axis else product_rows
                given = list(zip(firsts, arrays))
                return product(shares, starts, blocks, other, given, low, high - low, width, kind)

            source = self.shares
            return lane(compute, source.shares, source.starts, source.blocks, self.other_side, *arrays)

        def compute(whole, other, *arrays):
            part = whole[:, low * width : high * width]
            value = dot(other, part, TN) if axis else dot(part, other, TN)
            for first, array in zip(firsts, arrays):
                piece = lax.slice_in_dim(
                    array, (low - first) * width, (high - first) * width, axis=axis
                )
                value = value + piece.astype(WIDE)
            return value.astype(kind)

        return lane(compute, self.shares.array(), self.other_side, *arrays)

    def step(self, lane):
        sent = self.total(lane, self.low, self.low + self.size)
        self.low += self.size
        self.size //= 2
        self.got.append((self.low, swap(sent, "dp", self.masks.pop(0))))
        return self

    def finish(self, lane):
        while self.masks:
            self.step(lane)
        return self.total(lane, self.low, self.count)

    def step_half(self, lane):
        while len(self.masks) > 1:
            self.step(lane)
        sent = self.total(lane, self.low, self.low + self.size)
        self.low += self.size
        self.partner = swap(sent, "dp", self.masks.pop(0))
        return self

    def finish_half(self, lane, at):
        own = self.total(lane, self.low, self.count)
        return lane(lambda a, b, at: halves(a, b, at, 1 - self.axis), own, self.partner, at)


def rows_of(shares):
    return jnp.concatenate(shares, axis=0)


def inverse_rms(value_rows):
    return lax.rsqrt(jnp.mean(value_rows * value_rows, axis=-1, keepdims=True) + EPSILON)


def body(
    layer_in,
    cotangent,
    segments,
    gain_attn,
    w_query,
    key_weight,
    value_weight,
    w_out,
    gain_ffn,
    w_gate,
    w_up,
    w_down,
):
    share, width = layer_in.shape
    count = lax.axis_size("tensor")
    rank = lax.axis_index("tensor")
    place = lax.axis_index("dp")
    masks = powers(lax.axis_size("dp"))
    group_masks = [m for m in masks if m != PAIR] + [PAIR]
    at = place // PAIR % 2
    at_array = at.reshape(1).astype(jnp.int32)
    order = jnp.arange(count, dtype=jnp.int32) ^ rank
    seqs = segments.shape[0]
    q_width, kv_width = w_query.shape[1], key_weight.shape[1]
    rows = count * share
    lane = Lane()


    def first_norm(layer_in, gain):
        x = layer_in.astype(WIDE)
        inverse = inverse_rms(x)
        return (x * inverse * gain.astype(WIDE)).astype(LOW), inverse

    n1_own, inverse_one = lane(first_norm, layer_in, gain_attn)
    n1_far = swap(n1_own, "tensor", FAR)

    def prepare(segments, w_query, key_weight, value_weight, cotangent):
        tables = rope_tables(positions_of(segments).reshape(-1))
        w_qkv = jnp.concatenate([w_query, key_weight, value_weight], axis=1)
        seg_col, seg_row = segments.reshape(-1, 1), segments[:, None, :]
        branch_own = (RESIDUAL_SCALE * cotangent.astype(WIDE)).astype(LOW)
        return tables, w_qkv, seg_col, seg_row, branch_own

    tables, w_qkv, seg_col, seg_row, branch_own = lane(
        prepare, segments, w_query, key_weight, value_weight, cotangent
    )
    turned = q_width + kv_width
    qkv, n1_near = lane(
        lambda a, order, w, c, s: project(a, order, w, rows, NN, "near_in", turned, (c, s)),
        n1_own,
        order[:2],
        w_qkv,
        *tables,
    )
    n1_far = after(n1_far, qkv)
    branch_own = after(branch_own, n1_far)
    branch_chips = [
        branch_own,
        swap_both(branch_own),
        swap(branch_own, "tensor", FAR),
        swap(branch_own, "dp", PAIR),
    ]
    qkv, n1_other = lane(
        lambda a, order, w, c, s, q: project(a, order, w, rows, NN, "far_in", turned, (c, s), (q,)),
        n1_far,
        order[2:],
        w_qkv,
        *tables,
        qkv,
    )
    attended, lse = lane(
        lambda q, c, r: attend(q, q_width, kv_width, c, r, seqs), qkv, seg_col, seg_row
    )
    own_terms, far_terms = lane(
        lambda a, w, o: pieces(a, w, o, count, NN, "out_pieces"), attended, w_out, order
    )
    got_far = swap(lane(add_low, *far_terms), "tensor", FAR)

    branch_chips = after(tuple(branch_chips), *lane.last)
    branch_shares = [b for a in branch_chips for b in (a, swap(a, "tensor", NEAR))]
    d_mixed = lane(lambda a, w, at: branch(a, w, at), branch_shares, w_down, at_array)

    def second_norm(layer_in, mine, near, far, gain):
        hidden = layer_in.astype(WIDE) + RESIDUAL_SCALE * added(mine, near, far)
        inverse = inverse_rms(hidden)
        return hidden, inverse, (hidden * inverse * gain.astype(WIDE)).astype(LOW)

    hidden, inverse_two, n2_own = lane(
        second_norm, layer_in, *own_terms, got_far, gain_ffn
    )
    n2_far, n2_pair = swap(n2_own, "tensor", FAR), swap(n2_own, "dp", PAIR)
    n2_own = [n2_own, swap(n2_own, "tensor", NEAR)]
    blend = lambda block: lambda a, g, u, d, at, *m: mix(a, g, u, d, at, block, m)
    mixed = lane(blend(0), n2_own, w_gate, w_up, d_mixed, at_array)
    n2_far, n2_pair = after((n2_far, n2_pair), mixed)
    n2_both = [swap(cut(n2_pair)[0], "tensor", FAR), swap(cut(n2_far)[1], "dp", PAIR)]
    n2_four = [n2_far, swap(n2_far, "tensor", NEAR), n2_pair, swap(n2_pair, "tensor", NEAR)]
    mixed = lane(blend(1), n2_four, w_gate, w_up, d_mixed, at_array, *mixed)
    n2_both = list(after(tuple(n2_both), *lane.last))
    n2_both = n2_both + [swap(a, "tensor", NEAR) for a in n2_both]
    mixed, d_gate, d_upper = lane(blend(1), n2_both, w_gate, w_up, d_mixed, at_array, *mixed)

    n2 = Shares(n2_own + n2_both + n2_four, group_masks, place)
    grad_down = Reduction(Shares(branch_shares, group_masks, place), mixed, group_masks, 1).step(lane)
    grad_down = Reduction(Shares(branch_shares, group_masks, place), mixed, group_masks, 1).step(lane)
    ffn_parts = lane(lambda m, w, at: down(m, w, at, share), mixed, w_down, at_array)
    dn_parts = lane(
        lambda dg, du, wg, wu, at: unmix(dg, du, wg, wu, at, share),
        d_gate,
        d_upper,
        w_gate,
        w_up,
        at_array,
    )
    d_normed = GroupSum()
    d_normed.start_both(lane, dn_parts[1])
    grad_gate = Reduction(n2, d_gate, group_masks, 0).step(lane)
    d_normed.start_far_pair(lane, dn_parts[0], dn_parts[2], dn_parts[3])
    grad_up = Reduction(n2, d_upper, group_masks, 0).step(lane)
    grad_down.step(lane)
    d_hidden, da_own, gain_two_part = lane(
        lambda c, h, i, g, *t: norm_back(c, h, i, g, t, WIDE),
        cotangent,
        hidden,
        inverse_two,
        gain_ffn,
        *d_normed.terms(),
    )
    da_far = swap(da_own, "tensor", FAR)
    n1_shares = [n1_own, n1_near, n1_far, n1_other]
    n1 = Shares(n1_shares, masks, place, order)
    d_attn, da_near = lane(
        lambda a, o, w: project(a, o, w, rows, NT, "near_back"), da_own, order[:2], w_out
    )
    grad_gate.step(lane)
    d_attn, da_other = lane(
        lambda a, o, w, d: project(a, o, w, rows, NT, "far_back", given=(d,)),
        da_far,
        order[2:],
        w_out,
        d_attn,
    )
    out_total = GroupSum()
    out_total.start_both(lane, ffn_parts[1])
    grad_down.step_half(lane)
    d_qkv = lane(
        lambda q, g, l, c, r, a, b: attend_back(q, q_width, kv_width, g, l, c, r, a, b, seqs),
        qkv,
        d_attn,
        lse,
        seg_col,
        seg_row,
        *tables,
    )
    out_total.start_far_pair(lane, ffn_parts[0], ffn_parts[2], ffn_parts[3])
    own_terms, far_terms = lane(
        lambda a, w, o: pieces(a, w, o, count, NT, "in_pieces"), d_qkv, w_qkv, order
    )
    grad_qkv = Reduction(n1, d_qkv, masks, 0).step(lane)
    got_far = swap(lane(add_low, *far_terms), "tensor", FAR)
    grad_gate.step_half(lane)
    grad_up.step(lane)
    da = Shares([da_own, da_near, da_far, da_other], masks, place, order)
    grad_wout = Reduction(da, attended, masks, 1).step(lane)
    grad_down = grad_down.finish_half(lane, at_array)
    grad_rows, _, gain_one_part = lane(
        lambda c, h, i, g, *t: norm_back(c, h, i, g, t, LOW),
        d_hidden,
        layer_in,
        inverse_one,
        gain_attn,
        *own_terms,
        got_far,
    )
    grad_gate = grad_gate.finish_half(lane, at_array)
    grad_qkv.step(lane)
    grad_up.step_half(lane)
    out_rows = lane(
        lambda hidden, *terms: whole(
            lambda hidden, *terms: (hidden + RESIDUAL_SCALE * added(*terms),),
            [(hidden.shape, LOW)],
            hidden,
            *terms,
        )[0],
        hidden,
        *out_total.terms(),
    )
    grad_wout.step(lane)
    grad_qkv.step(lane)
    grad_up = grad_up.finish_half(lane, at_array)
    grad_wout.step(lane)
    grad_qkv = grad_qkv.finish(lane)
    steps = [("tensor", m) for m in powers(count)] + [("dp", m) for m in masks]
    gains = lane(
        lambda a, b: sum_all(jnp.concatenate([a, b], axis=0), steps), gain_one_part, gain_two_part
    )
    block = width // lax.axis_size("dp")
    gains = lax.dynamic_slice_in_dim(gains, place * block, block, 1)
    grad_wout = grad_wout.finish(lane)
    return (
        out_rows,
        grad_rows,
        gains[0],
        grad_qkv[:, :q_width],
        grad_qkv[:, q_width : q_width + kv_width],
        grad_qkv[:, q_width + kv_width :],
        grad_wout,
        gains[1],
        grad_gate,
        grad_up,
        grad_down,
    )


def solution(mesh):
    return jax.shard_map(
        body,
        mesh=mesh,
        in_specs=(
            P(("dp", "tensor"), None),
            P(("dp", "tensor"), None),
            P("dp", None),
            P(),
            P(None, "tensor"),
            P(None, "tensor"),
            P(None, "tensor"),
            P("tensor", None),
            P(),
            P(None, "tensor"),
            P(None, "tensor"),
            P("tensor", None),
        ),
        out_specs=(
            P(("dp", "tensor"), None),
            P(("dp", "tensor"), None),
            P("dp"),
            P("dp", "tensor"),
            P("dp", "tensor"),
            P("dp", "tensor"),
            P("tensor", "dp"),
            P("dp"),
            P("dp", "tensor"),
            P("dp", "tensor"),
            P("tensor", "dp"),
        ),
        check_vma=False,
    )
```
